32 devices in a mesh: tm: 8 (over z, y), head: 4 (over x, core).
Axes of the slice: x: 2, y: 2, z: 4, core: 2. Of those that a mesh axis runs over, the one named last changes fastest.
Arguments:
- query_rows: bfloat16 [4096, 1536], P('tm', 'head'), may hold values from -5 to 5
- key_rows: bfloat16 [4096, 1536], P('tm', 'head'), may hold values from -5 to 5
- value_rows: bfloat16 [4096, 1536], P('tm', 'head'), may hold values from -6 to 6
- output_weight: bfloat16 [1536, 1536], P('head'), may hold values from -0.15625 to 0.15625
- output_grad: bfloat16 [4096, 1536], P('tm', 'head'), may hold values from -6 to 6
- anchor: int32 [8], replicated, may hold values from 0 to 7, as said below
Outputs:
- layer_output: bfloat16 [4096, 1536], P('tm', 'head')
- query_grad: bfloat16 [4096, 1536], P('tm', 'head')
- key_grad: bfloat16 [4096, 1536], P('tm', 'head')
- value_grad: bfloat16 [4096, 1536], P('tm', 'head')
- weight_grad: float32 [1536, 1536], P('head')
The draws below stay inside these ranges and needn't reach their ends.
Inputs may be any that keep to these rules, and one draw needn't show every extreme that they name: anchor[0] = 0; anchor[f] is f or anchor[f - 1]; f - anchor[f] is below 4; the segment that starts at frame 8 // 2 - 2 has exactly 4 frames.
All inputs are finite; a program needn't handle non-finite values.
Results may differ from the reference program's by a relative error of at most 0.0083.
Values may be sent and summed in bfloat16 or wider, within the bound.
No kernel may reach another device: no remote copies, remote signals or barrier semaphores. Data moves between devices by JAX's collectives and lax.ppermute only.
A program may use at most 128 MiB of HBM per device.

```python
import jax
import jax.numpy as jnp
from jax import lax

HEADS = 12
HEAD_DIM = 128
D = 1536
LAT = 512
FRAMES = 8
SEG = 4
TOKENS = 4096


def base_field(key):
    return jnp.clip(jax.random.normal(key, (TOKENS, D), jnp.float32), -5.0, 5.0)


def draw_query_rows(key, part):
    field = base_field(jax.random.fold_in(key, 11))
    return field.astype(jnp.bfloat16)


def draw_key_rows(key, part):
    field = base_field(jax.random.fold_in(key, 13))
    return field.astype(jnp.bfloat16)


def draw_anchor(key, part):
    frame_ids = jnp.arange(FRAMES, dtype=jnp.int32)
    forced = FRAMES // 2 - 2
    after = forced + SEG
    first_lengths = jax.random.randint(jax.random.fold_in(key, 3), (FRAMES,), 1, SEG + 1)
    second_lengths = jax.random.randint(jax.random.fold_in(key, 5), (FRAMES,), 1, SEG + 1)
    first_starts = jnp.cumsum(first_lengths) - first_lengths
    second_starts = after + jnp.cumsum(second_lengths) - second_lengths
    first_ok = first_starts < forced
    first_pick = jnp.where(first_ok[None, :] & (first_starts[None, :] <= frame_ids[:, None]), first_starts[None, :], 0)
    second_pick = jnp.where(second_starts[None, :] <= frame_ids[:, None], second_starts[None, :], 0)
    forced_pick = jnp.where(frame_ids >= forced, forced, 0)
    computed = jnp.maximum(jnp.max(first_pick, axis=1), jnp.max(second_pick, axis=1))
    computed = jnp.maximum(computed, forced_pick)
    return computed.astype(jnp.int32)


def block_scale(own_key, shape, cuts, smallest, high):
    def one(dim, shards_of):
        steps = jax.random.uniform(jax.random.fold_in(jax.random.fold_in(own_key, 6), dim), (shards_of,), jnp.float32, smallest / len(cuts), high / len(cuts))
        return jnp.repeat(jnp.exp(steps), shape[dim] // shards_of).reshape((-1,) + (1,) * (len(shape) - dim - 1))

    factor_of = one(*cuts[0])
    for cut in cuts[1:]:
        factor_of = factor_of * one(*cut)
    return factor_of


def centred(stream_key, dims, width, reach, cuts=(), kind=jnp.bfloat16):
    values = jax.random.normal(stream_key, dims, jnp.float32) * width
    if len(cuts) > 0:
        values = block_scale(stream_key, dims, cuts, -0.22, 0.18) * values
    return jnp.clip(values, min=-reach, max=reach).astype(kind)


def setup_inputs(seed: int = 0) -> dict:
    arg_keys = jax.random.split(jax.random.key(seed), 7)
    return {
        "query_rows": draw_query_rows(jax.random.fold_in(arg_keys[6], 71), 0),
        "key_rows": draw_key_rows(jax.random.fold_in(arg_keys[6], 71), 0),
        "value_rows": centred(arg_keys[2], (TOKENS, D), 1.0, 6.0, ((0, 8), (1, 4))),
        "output_weight": centred(arg_keys[3], (D, D), D ** -0.5, 0.15625, ((0, 4),)),
        "output_grad": centred(arg_keys[4], (TOKENS, D), 1.0, 6.0, ((0, 8), (1, 4))),
        "anchor": draw_anchor(jax.random.fold_in(arg_keys[6], 71), 0),
    }


def reference(query_rows, key_rows, value_rows, output_weight, output_grad, anchor):
    scaling = HEAD_DIM ** -0.5

    def frame_rows(array, frame_index):
        return lax.dynamic_slice_in_dim(array, (frame_index * LAT).astype(jnp.int32), LAT, 0)

    def frame_step(running, frame_index):
        key_total, value_total, weight_total = running
        anchor_frame = anchor[frame_index].astype(jnp.int32)
        previous = jnp.where(anchor_frame < frame_index, frame_index - 1, frame_index).astype(jnp.int32)
        sources = (anchor_frame, previous, frame_index)
        queries = frame_rows(query_rows, frame_index).astype(jnp.float32).reshape(LAT, HEADS, HEAD_DIM)
        gathered_keys = jnp.concatenate([frame_rows(key_rows, source) for source in sources], 0)
        gathered_keys = gathered_keys.astype(jnp.float32).reshape(3 * LAT, HEADS, HEAD_DIM)
        gathered_values = jnp.concatenate([frame_rows(value_rows, source) for source in sources], 0)
        gathered_values = gathered_values.astype(jnp.float32).reshape(3 * LAT, HEADS, HEAD_DIM)
        scores = jnp.einsum("qhd,khd->hqk", queries, gathered_keys) * scaling
        highest = jnp.max(scores, axis=-1, keepdims=True)
        raw_weights = jnp.exp(scores - highest)
        probabilities = raw_weights / jnp.sum(raw_weights, axis=-1, keepdims=True)
        rounded = lax.optimization_barrier(probabilities.astype(jnp.bfloat16)).astype(jnp.float32)
        attended = jnp.einsum("hqk,khd->qhd", rounded, gathered_values).astype(jnp.bfloat16).reshape(LAT, D)
        layer_rows = jnp.dot(attended, output_weight, preferred_element_type=jnp.float32).astype(jnp.bfloat16)
        grad_rows = frame_rows(output_grad, frame_index)
        attended_grad = jnp.dot(grad_rows, output_weight.T, preferred_element_type=jnp.float32).astype(jnp.bfloat16)
        weight_total = weight_total + jnp.dot(attended.T, grad_rows, preferred_element_type=jnp.float32)
        grad_heads = lax.optimization_barrier(attended_grad).astype(jnp.float32).reshape(LAT, HEADS, HEAD_DIM)
        value_blocks = jnp.einsum("hqk,qhd->khd", rounded, grad_heads).reshape(3 * LAT, D)
        prob_grad = jnp.einsum("qhd,khd->hqk", grad_heads, gathered_values)
        row_delta = jnp.sum(probabilities * prob_grad, axis=-1, keepdims=True)
        score_grad = (probabilities * (prob_grad - row_delta) * scaling).astype(jnp.bfloat16)
        score_grad = lax.optimization_barrier(score_grad).astype(jnp.float32)
        query_block = jnp.einsum("hqk,khd->qhd", score_grad, gathered_keys).astype(jnp.bfloat16).reshape(LAT, D)
        key_blocks = jnp.einsum("hqk,qhd->khd", score_grad, queries).reshape(3 * LAT, D)
        for block_index in range(3):
            offset = (sources[block_index] * LAT).astype(jnp.int32)
            key_part = key_blocks[block_index * LAT:(block_index + 1) * LAT]
            value_part = value_blocks[block_index * LAT:(block_index + 1) * LAT]
            key_total = lax.dynamic_update_slice_in_dim(
                key_total, lax.dynamic_slice_in_dim(key_total, offset, LAT, 0) + key_part, offset, 0)
            value_total = lax.dynamic_update_slice_in_dim(
                value_total, lax.dynamic_slice_in_dim(value_total, offset, LAT, 0) + value_part, offset, 0)
        return (key_total, value_total, weight_total), (layer_rows, query_block)

    initial = (jnp.zeros((TOKENS, D), jnp.float32), jnp.zeros((TOKENS, D), jnp.float32),
               jnp.zeros((D, D), jnp.float32))
    running, stacked = lax.scan(frame_step, initial, jnp.arange(FRAMES, dtype=jnp.int32))
    key_total, value_total, weight_total = running
    layer_rows, query_block = stacked
    return (layer_rows.reshape(TOKENS, D), query_block.reshape(TOKENS, D),
            key_total.astype(jnp.bfloat16), value_total.astype(jnp.bfloat16), weight_total)
```

```python
import functools
import math

import jax
import jax.numpy as jnp
from jax import lax
from jax.experimental import pallas as pl
from jax.experimental.pallas import tpu as pltpu
from jax.sharding import PartitionSpec as P

HEAD_DIM = 128
BF16 = jnp.bfloat16
F32 = jnp.float32
SCALE = HEAD_DIM ** -0.5
SCALE_LOG2 = SCALE * math.log2(math.e)
Q_CHUNK = 256


def dot(a, b, dims):
    return lax.dot_general(a, b, (dims, ((), ())), preferred_element_type=F32)


def anchor_bounds(frames, seg):
    forced = frames // 2 - 2
    bounds = []
    for f in range(frames):
        if f < forced:
            bounds.append((max(0, f - seg + 1), f))
        elif f < forced + seg:
            bounds.append((forced, forced))
        else:
            bounds.append((max(forced + seg, f - seg + 1), f))
    return bounds


def vmem():
    return pl.BlockSpec(memory_space=pltpu.VMEM)


def smem():
    return pl.BlockSpec(memory_space=pltpu.SMEM)


def params():
    return pltpu.CompilerParams(vmem_limit_bytes=48 * 1024 * 1024)


def cotangent_kernel(own, across, beside, weight, out):
    head = lax.axis_index("head")
    width = own.shape[1]
    pieces = (own[...], beside[0], across[...], beside[1])
    total = None
    for m, piece in enumerate(pieces):
        start = pl.multiple_of((head ^ m) * width, 128)
        term = dot(piece, weight[:, pl.ds(start, width)], ((1,), (1,)))
        total = term if total is None else total + term
    out[...] = total.astype(BF16)


def gather_block(anchor, own, prev, far, extra_ref, kind):
    f = lax.axis_index("tm")
    a = anchor[f]
    mine = own[...]
    before = jnp.where(a < f, prev[kind], mine)
    distant = far[kind]
    if extra_ref is not None:
        distant = distant + extra_ref[...]
    first = jnp.where(f - a >= 2, distant, before)
    return first, before, mine


def forward_kernel(extra, anchor, q, k, v, prev, far, *rest):
    extra_k, extra_v = rest[:2] if extra else (None, None)
    grad, out, out_t, stats, keys, values = rest[2 if extra else 0 :]
    rows = q.shape[0]
    for block, part in enumerate(gather_block(anchor, k, prev, far, extra_k, 0)):
        keys[pl.ds(block * rows, rows), :] = part
    for block, part in enumerate(gather_block(anchor, v, prev, far, extra_v, 1)):
        values[pl.ds(block * rows, rows), :] = part
    for c in range(rows // Q_CHUNK):
        at = pl.ds(c * Q_CHUNK, Q_CHUNK)
        scores = dot(keys[...], q[at, :], ((1,), (1,)))
        highest = jnp.max(scores, axis=0, keepdims=True)
        raw = jnp.exp2((scores - highest) * SCALE_LOG2)
        total = jnp.sum(raw, axis=0, keepdims=True)
        attended = dot(values[...], raw.astype(BF16), ((0,), (0,))) / total
        out_t[:, at] = attended.astype(BF16)
        out[at, :] = attended.T.astype(BF16)
        delta = jnp.sum(attended * grad[at, :].astype(F32).T, axis=0, keepdims=True)
        stats[0, 0:1, at] = highest * SCALE_LOG2 + jnp.log2(total)
        stats[0, 1:2, at] = delta


def backward_kernel(extra, anchor, q, k, v, prev, far, *rest):
    extra_k, extra_v = rest[:2] if extra else (None, None)
    grad, stats, dq, own_grad, prev_grad, far_grad, keys, values, dk, dv = rest[2 if extra else 0 :]
    rows = q.shape[0]
    for block, part in enumerate(gather_block(anchor, k, prev, far, extra_k, 0)):
        keys[pl.ds(block * rows, rows), :] = part
    for block, part in enumerate(gather_block(anchor, v, prev, far, extra_v, 1)):
        values[pl.ds(block * rows, rows), :] = part
    for c in range(rows // Q_CHUNK):
        at = pl.ds(c * Q_CHUNK, Q_CHUNK)
        queries, cot = q[at, :], grad[at, :]
        scores = dot(keys[...], queries, ((1,), (1,)))
        prob = jnp.exp2(scores * SCALE_LOG2 - stats[0, 0:1, at])
        prob_grad = dot(values[...], cot, ((1,), (1,)))
        score_grad = (prob * (prob_grad - stats[0, 1:2, at])).astype(BF16)
        dv_term = dot(prob.astype(BF16), cot, ((1,), (0,)))
        dk_term = dot(score_grad, queries, ((1,), (0,)))
        if c == 0:
            dv[...] = dv_term
            dk[...] = dk_term
        else:
            dv[...] += dv_term
            dk[...] += dk_term
        dq_t = dot(keys[...], score_grad, ((0,), (0,))) * SCALE
        dq[at, :] = dq_t.T.astype(BF16)
    f = lax.axis_index("tm")
    a = anchor[f]
    for kind, (ref, factor) in enumerate(((dk, SCALE), (dv, None))):
        parts = [ref[pl.ds(block * rows, rows), :] for block in range(3)]
        if factor is not None:
            parts = [part * factor for part in parts]
        near = parts[1] + jnp.where(f - a >= 2, 0.0, parts[0])
        far_grad[kind] = jnp.where(f - a >= 2, parts[0], 0.0).astype(BF16)
        prev_grad[kind] = jnp.where(a < f, near, 0.0).astype(BF16)
        own_grad[kind] = parts[2] + jnp.where(a < f, 0.0, near)


def projection_kernel(attended_t, own, across, beside, keep, send, pieces):
    tm = lax.axis_index("tm")
    sel = (tm % 2) * 2 + (tm // 2) % 2
    pieces[0] = own[...]
    pieces[1] = beside[0]
    pieces[2] = across[...]
    pieces[3] = beside[1]
    for slot in range(4):
        term = dot(attended_t[...], pieces[slot ^ sel], ((1,), (0,)))
        if slot < 2:
            keep[slot] = term
        else:
            send[slot - 2] = term.astype(BF16)


def output_kernel(attended, weight, keep, send):
    head = lax.axis_index("head")
    width = weight.shape[0]
    for m in range(4):
        start = pl.multiple_of((head ^ m) * width, 128)
        part = dot(attended[...], weight[:, pl.ds(start, width)], ((1,), (0,)))
        if m % 2:
            send[m // 2] = part.astype(BF16)
        else:
            keep[m // 2] = part


def assemble_kernel(first, second, others, out):
    head = lax.axis_index("head")
    tm = lax.axis_index("tm")
    sel = (tm % 2) * 2 + (tm // 2) % 2
    width = first.shape[0]
    for slot in range(4):
        value = (first[...], second[...], others[0], others[1])[slot]
        start = pl.multiple_of((head ^ sel ^ slot) * width, 128)
        out[:, pl.ds(start, width)] = value.astype(out.dtype)


def swap(array, axis, bit):
    return lax.ppermute(array, axis, [(i, i ^ bit) for i in range(lax.axis_size(axis))])


def local(query_rows, key_rows, value_rows, output_weight, output_grad, anchor):
    rows, cols = query_rows.shape
    heads = cols // HEAD_DIM
    frames = lax.axis_size("tm")
    seg = min(8, frames // 2)
    bounds = anchor_bounds(frames, seg)
    position = lax.axis_index("tm")
    near_pairs = [(f - 1, f) for f in range(1, frames) if bounds[f][0] < f]
    far_frames = [f for f in range(frames) if f - bounds[f][0] >= 2]
    pair_plan = len(far_frames) == 2 and all(bounds[f][0] == bounds[f][1] for f in far_frames)

    def send(array, pairs):
        return lax.ppermute(array, "tm", pairs)

    def back(pairs):
        return [(b, a) for a, b in pairs]

    own_pair = jnp.stack([key_rows, value_rows])
    prev_pair = send(own_pair, near_pairs)
    if pair_plan:
        lower, upper = far_frames
        source = bounds[lower][0]
        far_pair = send(own_pair, [(source, lower)])
        extra = (send(key_rows, [(source, upper)]), send(prev_pair[1], [(source + 1, upper)]))
    else:
        own_anchor = jnp.sum(jnp.where(jnp.arange(frames) == position, anchor, 0))
        distance = position - own_anchor
        far_pair = jnp.where(distance == 0, own_pair, prev_pair)
        step = 2
        while step < seg:
            pairs = [(f - step, f) for f in range(step, frames) if f - bounds[f][0] >= step]
            far_pair = jnp.where(distance >= step, send(far_pair, pairs), far_pair)
            step *= 2
        extra = ()

    across = swap(output_grad, "head", 2)
    beside = swap(jnp.stack([output_grad, across]), "head", 1)
    attended_grad = pl.pallas_call(
        cotangent_kernel,
        out_shape=jax.ShapeDtypeStruct((rows, cols), BF16),
        in_specs=[vmem()] * 4,
        out_specs=vmem(),
        compiler_params=params(),
        name="cotangent",
    )(output_grad, across, beside, output_weight)

    by_head = pl.BlockSpec((rows, HEAD_DIM), lambda h: (0, h))
    pair_by_head = pl.BlockSpec((2, rows, HEAD_DIM), lambda h: (0, 0, h))
    stat_spec = pl.BlockSpec((1, 8, rows), lambda h: (h, 0, 0))
    sources = [smem(), by_head, by_head, by_head, pair_by_head, pair_by_head] + [by_head] * len(extra)
    blocks = [pltpu.VMEM((3 * rows, HEAD_DIM), BF16)] * 2
    gathered = (anchor, query_rows, key_rows, value_rows, prev_pair, far_pair, *extra)
    attended, attended_t, stats = pl.pallas_call(
        functools.partial(forward_kernel, bool(extra)),
        grid=(heads,),
        out_shape=(
            jax.ShapeDtypeStruct((rows, cols), BF16),
            jax.ShapeDtypeStruct((cols, rows), BF16),
            jax.ShapeDtypeStruct((heads, 8, rows), F32),
        ),
        in_specs=[*sources, by_head],
        out_specs=(by_head, pl.BlockSpec((HEAD_DIM, rows), lambda h: (h, 0)), stat_spec),
        scratch_shapes=blocks,
        compiler_params=params(),
        name="forward",
    )(*gathered, attended_grad)

    keep, away = pl.pallas_call(
        projection_kernel,
        out_shape=(
            jax.ShapeDtypeStruct((2, cols, cols), F32),
            jax.ShapeDtypeStruct((2, cols, cols), BF16),
        ),
        in_specs=[vmem()] * 4,
        out_specs=(vmem(), vmem()),
        scratch_shapes=[pltpu.VMEM((4, rows, cols), BF16)],
        compiler_params=params(),
        name="projection",
    )(attended_t, output_grad, across, beside)

    query_grad, own_grad, prev_grad, far_grad = pl.pallas_call(
        functools.partial(backward_kernel, bool(extra)),
        grid=(heads,),
        out_shape=(
            jax.ShapeDtypeStruct((rows, cols), BF16),
            jax.ShapeDtypeStruct((2, rows, cols), F32),
            jax.ShapeDtypeStruct((2, rows, cols), BF16),
            jax.ShapeDtypeStruct((2, rows, cols), BF16),
        ),
        in_specs=[*sources, by_head, stat_spec],
        out_specs=(by_head, pair_by_head, pair_by_head, pair_by_head),
        scratch_shapes=blocks + [pltpu.VMEM((3 * rows, HEAD_DIM), F32)] * 2,
        compiler_params=params(),
        name="backward",
    )(*gathered, attended_grad, stats)

    if frames == 8:
        half = keep + swap(away, "tm", 1).astype(F32)
        quarter = (half[0] + swap(half[1].astype(BF16), "tm", 2).astype(F32)).astype(BF16)
        first = (quarter.astype(F32) + swap(quarter, "tm", 4).astype(F32)).astype(BF16)
        second = swap(first, "tm", 2)
        others = swap(jnp.stack([first, second]), "tm", 1)
    else:
        first, second, others = keep[0], keep[1], away.astype(F32)
    weight_grad = pl.pallas_call(
        assemble_kernel,
        out_shape=jax.ShapeDtypeStruct((cols, 4 * cols), F32),
        in_specs=[vmem()] * 3,
        out_specs=vmem(),
        compiler_params=params(),
        name="assemble",
    )(first, second, others)
    if frames != 8:
        weight_grad = lax.psum(weight_grad, "tm")

    if pair_plan:
        crossing = send(
            jnp.where(position == lower, far_grad[1], far_grad[0]), [(lower, upper), (upper, lower)]
        )
        far_keys = (far_grad[0].astype(F32) + crossing.astype(F32)).astype(BF16)
        far_values = (far_grad[1].astype(F32) + crossing.astype(F32)).astype(BF16)
        from_far = jnp.stack(
            [send(far_keys, [(lower, source)]), send(far_values, [(upper, source)])]
        ).astype(F32)
        from_near = send(prev_grad, back(near_pairs)).astype(F32)
        totals = own_grad + from_near + from_far
    else:
        held = far_grad.astype(F32)
        while step > 2:
            step //= 2
            pairs = [(f, f - step) for f in range(step, frames) if f - bounds[f][0] >= step]
            leaving = jnp.where(distance >= step, held, 0.0)
            held = (held - leaving) + send(leaving.astype(BF16), pairs).astype(F32)
        to_prev = prev_grad.astype(F32) + jnp.where(distance == 1, held, 0.0)
        from_near = send(to_prev.astype(BF16), back(near_pairs)).astype(F32)
        totals = own_grad + from_near + jnp.where(distance == 0, held, 0.0)
    key_grad, value_grad = totals[0].astype(BF16), totals[1].astype(BF16)

    out_keep, out_send = pl.pallas_call(
        output_kernel,
        out_shape=(
            jax.ShapeDtypeStruct((2, rows, cols), F32),
            jax.ShapeDtypeStruct((2, rows, cols), BF16),
        ),
        in_specs=[vmem()] * 2,
        out_specs=(vmem(), vmem()),
        compiler_params=params(),
        name="output",
    )(attended, output_weight)
    pair_sum = out_keep + swap(out_send, "head", 1).astype(F32)
    layer_output = (pair_sum[0] + swap(pair_sum[1].astype(BF16), "head", 2).astype(F32)).astype(BF16)
    return layer_output, query_grad, key_grad, value_grad, weight_grad


def solution(mesh):
    in_specs = (
        P("tm", "head"),
        P("tm", "head"),
        P("tm", "head"),
        P("head", None),
        P("tm", "head"),
        P(),
    )
    out_specs = (
        P("tm", "head"),
        P("tm", "head"),
        P("tm", "head"),
        P("tm", "head"),
        P("head", None),
    )
    return jax.shard_map(local, mesh=mesh, in_specs=in_specs, out_specs=out_specs, check_vma=False)
```

```python
import functools
import math

import jax
import jax.numpy as jnp
from jax import lax
from jax.experimental import pallas as pl
from jax.experimental.pallas import tpu as pltpu
from jax.sharding import PartitionSpec as P

HEAD_DIM = 128
BF16 = jnp.bfloat16
F32 = jnp.float32
SCALE = HEAD_DIM ** -0.5
SCALE_LOG2 = SCALE * math.log2(math.e)
Q_CHUNK = 256


def dot(a, b, dims):
    return lax.dot_general(a, b, (dims, ((), ())), preferred_element_type=F32)


def anchor_bounds(frames, seg):
    forced = frames // 2 - 2
    bounds = []
    for f in range(frames):
        if f < forced:
            bounds.append((max(0, f - seg + 1), f))
        elif f < forced + seg:
            bounds.append((forced, forced))
        else:
            bounds.append((max(forced + seg, f - seg + 1), f))
    return bounds


def vmem():
    return pl.BlockSpec(memory_space=pltpu.VMEM)


def smem():
    return pl.BlockSpec(memory_space=pltpu.SMEM)


def params(mebibytes):
    return pltpu.CompilerParams(vmem_limit_bytes=mebibytes * 1024 * 1024)


def cotangent_kernel(own, second, third, fourth, weight, out):
    head = lax.axis_index("head")
    width = own.shape[1]
    total = None
    for m, piece in enumerate((own, second, third, fourth)):
        start = pl.multiple_of((head ^ m) * width, 128)
        term = dot(piece[...], weight[:, pl.ds(start, width)], ((1,), (1,)))
        total = term if total is None else total + term
    out[...] = total.astype(BF16)


def gather_block(anchor, own, prev, far, extra_ref, kind):
    f = lax.axis_index("tm")
    a = anchor[f]
    mine = own[...]
    before = jnp.where(a < f, prev[kind], mine)
    distant = far[kind]
    if extra_ref is not None:
        distant = distant + extra_ref[...]
    first = jnp.where(f - a >= 2, distant, before)
    return first, before, mine


def forward_kernel(extra, anchor, q, k, v, prev, far, *rest):
    extra_k, extra_v = rest[:2] if extra else (None, None)
    grad, out, out_t, stats, keys, values = rest[2 if extra else 0 :]
    rows = q.shape[0]
    for block, part in enumerate(gather_block(anchor, k, prev, far, extra_k, 0)):
        keys[pl.ds(block * rows, rows), :] = part
    for block, part in enumerate(gather_block(anchor, v, prev, far, extra_v, 1)):
        values[pl.ds(block * rows, rows), :] = part
    for c in range(rows // Q_CHUNK):
        at = pl.ds(c * Q_CHUNK, Q_CHUNK)
        scores = dot(keys[...], q[at, :], ((1,), (1,)))
        highest = jnp.max(scores, axis=0, keepdims=True)
        raw = jnp.exp2((scores - highest) * SCALE_LOG2)
        total = jnp.sum(raw, axis=0, keepdims=True)
        attended = dot(values[...], raw.astype(BF16), ((0,), (0,))) / total
        out_t[:, at] = attended.astype(BF16)
        out[at, :] = attended.T.astype(BF16)
        delta = jnp.sum(attended * grad[at, :].astype(F32).T, axis=0, keepdims=True)
        stats[0, 0:1, at] = highest * SCALE_LOG2 + jnp.log2(total)
        stats[0, 1:2, at] = delta


def backward_kernel(extra, anchor, q, k, v, prev, far, *rest):
    extra_k, extra_v = rest[:2] if extra else (None, None)
    grad, stats, dq, own_grad, prev_grad, far_grad, keys, values, dk, dv = rest[2 if extra else 0 :]
    rows = q.shape[0]
    for block, part in enumerate(gather_block(anchor, k, prev, far, extra_k, 0)):
        keys[pl.ds(block * rows, rows), :] = part
    for block, part in enumerate(gather_block(anchor, v, prev, far, extra_v, 1)):
        values[pl.ds(block * rows, rows), :] = part
    for c in range(rows // Q_CHUNK):
        at = pl.ds(c * Q_CHUNK, Q_CHUNK)
        queries, cot = q[at, :], grad[at, :]
        scores = dot(keys[...], queries, ((1,), (1,)))
        prob = jnp.exp2(scores * SCALE_LOG2 - stats[0, 0:1, at])
        prob_grad = dot(values[...], cot, ((1,), (1,)))
        score_grad = (prob * (prob_grad - stats[0, 1:2, at])).astype(BF16)
        dv_term = dot(prob.astype(BF16), cot, ((1,), (0,)))
        dk_term = dot(score_grad, queries, ((1,), (0,)))
        if c == 0:
            dv[...] = dv_term
            dk[...] = dk_term
        else:
            dv[...] += dv_term
            dk[...] += dk_term
        dq_t = dot(keys[...], score_grad, ((0,), (0,))) * SCALE
        dq[at, :] = dq_t.T.astype(BF16)
    f = lax.axis_index("tm")
    a = anchor[f]
    for kind, (ref, factor) in enumerate(((dk, SCALE), (dv, None))):
        parts = [ref[pl.ds(block * rows, rows), :] for block in range(3)]
        if factor is not None:
            parts = [part * factor for part in parts]
        near = parts[1] + jnp.where(f - a >= 2, 0.0, parts[0])
        far_grad[kind] = jnp.where(f - a >= 2, parts[0], 0.0).astype(BF16)
        prev_grad[kind] = jnp.where(a < f, near, 0.0).astype(BF16)
        own_grad[kind] = parts[2] + jnp.where(a < f, 0.0, near)


def projection_kernel(attended_t, own, second, third, fourth, keep, send, pieces):
    tm = lax.axis_index("tm")
    sel = (tm % 2) * 2 + (tm // 2) % 2
    for m, piece in enumerate((own, second, third, fourth)):
        pieces[m] = piece[...]
    for slot in range(4):
        term = dot(attended_t[...], pieces[slot ^ sel], ((1,), (0,)))
        if slot < 2:
            keep[slot] = term
        else:
            send[slot - 2] = term.astype(BF16)


def output_kernel(attended, weight, keep, send):
    head = lax.axis_index("head")
    width = weight.shape[0]
    for m in range(4):
        start = pl.multiple_of((head ^ m) * width, 128)
        part = dot(attended[...], weight[:, pl.ds(start, width)], ((1,), (0,)))
        if m % 2:
            send[m // 2] = part.astype(BF16)
        else:
            keep[m // 2] = part


def assemble_kernel(first, second, others, out):
    head = lax.axis_index("head")
    tm = lax.axis_index("tm")
    sel = (tm % 2) * 2 + (tm // 2) % 2
    width = first.shape[0]
    for slot in range(4):
        value = (first[...], second[...], others[0], others[1])[slot]
        start = pl.multiple_of((head ^ sel ^ slot) * width, 128)
        out[:, pl.ds(start, width)] = value.astype(out.dtype)


def swap(array, axis, bit):
    return lax.ppermute(array, axis, [(i, i ^ bit) for i in range(lax.axis_size(axis))])


def local(query_rows, key_rows, value_rows, output_weight, output_grad, anchor):
    rows, cols = query_rows.shape
    heads = cols // HEAD_DIM
    frames = lax.axis_size("tm")
    seg = min(8, frames // 2)
    bounds = anchor_bounds(frames, seg)
    position = lax.axis_index("tm")
    near_pairs = [(f - 1, f) for f in range(1, frames) if bounds[f][0] < f]
    far_frames = [f for f in range(frames) if f - bounds[f][0] >= 2]
    pair_plan = len(far_frames) == 2 and all(bounds[f][0] == bounds[f][1] for f in far_frames)

    def send(array, pairs):
        return lax.ppermute(array, "tm", pairs)

    def back(pairs):
        return [(b, a) for a, b in pairs]

    own_pair = jnp.stack([key_rows, value_rows])
    prev_pair = send(own_pair, near_pairs)
    if pair_plan:
        lower, upper = far_frames
        source = bounds[lower][0]
        far_pair = send(own_pair, [(source, lower)])
        extra = (send(key_rows, [(source, upper)]), send(prev_pair[1], [(source + 1, upper)]))
    else:
        own_anchor = jnp.sum(jnp.where(jnp.arange(frames) == position, anchor, 0))
        distance = position - own_anchor
        far_pair = jnp.where(distance == 0, own_pair, prev_pair)
        step = 2
        while step < seg:
            pairs = [(f - step, f) for f in range(step, frames) if f - bounds[f][0] >= step]
            far_pair = jnp.where(distance >= step, send(far_pair, pairs), far_pair)
            step *= 2
        extra = ()

    others = tuple(swap(output_grad, "head", m) for m in (1, 2, 3))
    attended_grad = pl.pallas_call(
        cotangent_kernel,
        out_shape=jax.ShapeDtypeStruct((rows, cols), BF16),
        in_specs=[vmem()] * 5,
        out_specs=vmem(),
        compiler_params=params(8),
        name="cotangent",
    )(output_grad, *others, output_weight)

    by_head = pl.BlockSpec((rows, HEAD_DIM), lambda h: (0, h))
    pair_by_head = pl.BlockSpec((2, rows, HEAD_DIM), lambda h: (0, 0, h))
    stat_spec = pl.BlockSpec((1, 8, rows), lambda h: (h, 0, 0))
    sources = [smem(), by_head, by_head, by_head, pair_by_head, pair_by_head] + [by_head] * len(extra)
    blocks = [pltpu.VMEM((3 * rows, HEAD_DIM), BF16)] * 2
    gathered = (anchor, query_rows, key_rows, value_rows, prev_pair, far_pair, *extra)
    attended, attended_t, stats = pl.pallas_call(
        functools.partial(forward_kernel, bool(extra)),
        grid=(heads,),
        out_shape=(
            jax.ShapeDtypeStruct((rows, cols), BF16),
            jax.ShapeDtypeStruct((cols, rows), BF16),
            jax.ShapeDtypeStruct((heads, 8, rows), F32),
        ),
        in_specs=[*sources, by_head],
        out_specs=(by_head, pl.BlockSpec((HEAD_DIM, rows), lambda h: (h, 0)), stat_spec),
        scratch_shapes=blocks,
        compiler_params=params(24),
        name="forward",
    )(*gathered, attended_grad)

    keep, away = pl.pallas_call(
        projection_kernel,
        out_shape=(
            jax.ShapeDtypeStruct((2, cols, cols), F32),
            jax.ShapeDtypeStruct((2, cols, cols), BF16),
        ),
        in_specs=[vmem()] * 5,
        out_specs=(vmem(), vmem()),
        scratch_shapes=[pltpu.VMEM((4, rows, cols), BF16)],
        compiler_params=params(8),
        name="projection",
    )(attended_t, output_grad, *others)

    query_grad, own_grad, prev_grad, far_grad = pl.pallas_call(
        functools.partial(backward_kernel, bool(extra)),
        grid=(heads,),
        out_shape=(
            jax.ShapeDtypeStruct((rows, cols), BF16),
            jax.ShapeDtypeStruct((2, rows, cols), F32),
            jax.ShapeDtypeStruct((2, rows, cols), BF16),
            jax.ShapeDtypeStruct((2, rows, cols), BF16),
        ),
        in_specs=[*sources, by_head, stat_spec],
        out_specs=(by_head, pair_by_head, pair_by_head, pair_by_head),
        scratch_shapes=blocks + [pltpu.VMEM((3 * rows, HEAD_DIM), F32)] * 2,
        compiler_params=params(24),
        name="backward",
    )(*gathered, attended_grad, stats)

    if frames == 8:
        half = keep + swap(away, "tm", 1).astype(F32)
        quarter = (half[0] + swap(half[1].astype(BF16), "tm", 2).astype(F32)).astype(BF16)
        first = (quarter.astype(F32) + swap(quarter, "tm", 4).astype(F32)).astype(BF16)
        second = swap(first, "tm", 2)
        last = swap(jnp.stack([first, second]), "tm", 1)
    else:
        first, second, last = keep[0], keep[1], away.astype(F32)
    weight_grad = pl.pallas_call(
        assemble_kernel,
        out_shape=jax.ShapeDtypeStruct((cols, 4 * cols), F32),
        in_specs=[vmem()] * 3,
        out_specs=vmem(),
        compiler_params=params(8),
        name="assemble",
    )(first, second, last)
    if frames != 8:
        weight_grad = lax.psum(weight_grad, "tm")

    if pair_plan:
        crossing = send(
            jnp.where(position == lower, far_grad[1], far_grad[0]), [(lower, upper), (upper, lower)]
        )
        far_keys = (far_grad[0].astype(F32) + crossing.astype(F32)).astype(BF16)
        far_values = (far_grad[1].astype(F32) + crossing.astype(F32)).astype(BF16)
        from_far = jnp.stack(
            [send(far_keys, [(lower, source)]), send(far_values, [(upper, source)])]
        ).astype(F32)
        from_near = send(prev_grad, back(near_pairs)).astype(F32)
        totals = own_grad + from_near + from_far
    else:
        held = far_grad.astype(F32)
        while step > 2:
            step //= 2
            pairs = [(f, f - step) for f in range(step, frames) if f - bounds[f][0] >= step]
            leaving = jnp.where(distance >= step, held, 0.0)
            held = (held - leaving) + send(leaving.astype(BF16), pairs).astype(F32)
        to_prev = prev_grad.astype(F32) + jnp.where(distance == 1, held, 0.0)
        from_near = send(to_prev.astype(BF16), back(near_pairs)).astype(F32)
        totals = own_grad + from_near + jnp.where(distance == 0, held, 0.0)
    key_grad, value_grad = totals[0].astype(BF16), totals[1].astype(BF16)

    out_keep, out_send = pl.pallas_call(
        output_kernel,
        out_shape=(
            jax.ShapeDtypeStruct((2, rows, cols), F32),
            jax.ShapeDtypeStruct((2, rows, cols), BF16),
        ),
        in_specs=[vmem()] * 2,
        out_specs=(vmem(), vmem()),
        compiler_params=params(8),
        name="output",
    )(attended, output_weight)
    pair_sum = out_keep + swap(out_send, "head", 1).astype(F32)
    layer_output = (pair_sum[0] + swap(pair_sum[1].astype(BF16), "head", 2).astype(F32)).astype(BF16)
    return layer_output, query_grad, key_grad, value_grad, weight_grad


def solution(mesh):
    in_specs = (
        P("tm", "head"),
        P("tm", "head"),
        P("tm", "head"),
        P("head", None),
        P("tm", "head"),
        P(),
    )
    out_specs = (
        P("tm", "head"),
        P("tm", "head"),
        P("tm", "head"),
        P("tm", "head"),
        P("head", None),
    )
    return jax.shard_map(local, mesh=mesh, in_specs=in_specs, out_specs=out_specs, check_vma=False)
```

```python
import functools
import math

import jax
import jax.numpy as jnp
from jax import lax
from jax.experimental import pallas as pl
from jax.experimental.pallas import tpu as pltpu
from jax.sharding import PartitionSpec as P

HEAD_DIM = 128
BF16 = jnp.bfloat16
F32 = jnp.float32
SCALE = HEAD_DIM ** -0.5
SCALE_LOG2 = SCALE * math.log2(math.e)
Q_CHUNK = 256


def dot(a, b, dims):
    return lax.dot_general(a, b, (dims, ((), ())), preferred_element_type=F32)


def anchor_bounds(frames, seg):
    forced = frames // 2 - 2
    bounds = []
    for f in range(frames):
        if f < forced:
            bounds.append((max(0, f - seg + 1), f))
        elif f < forced + seg:
            bounds.append((forced, forced))
        else:
            bounds.append((max(forced + seg, f - seg + 1), f))
    return bounds


def vmem():
    return pl.BlockSpec(memory_space=pltpu.VMEM)


def smem():
    return pl.BlockSpec(memory_space=pltpu.SMEM)


def params(mebibytes):
    return pltpu.CompilerParams(vmem_limit_bytes=mebibytes * 1024 * 1024)


def cotangent_kernel(own, second, third, fourth, weight, out):
    head = lax.axis_index("head")
    width = own.shape[1]
    total = None
    for m, piece in enumerate((own, second, third, fourth)):
        start = pl.multiple_of((head ^ m) * width, 128)
        term = dot(piece[...], weight[:, pl.ds(start, width)], ((1,), (1,)))
        total = term if total is None else total + term
    out[...] = total.astype(BF16)


def earlier(anchor, own, prev):
    f = lax.axis_index("tm")
    return jnp.where(anchor[f] < f, prev, own[...])


def furthest(anchor, own, prev, far):
    f = lax.axis_index("tm")
    distant = far[0]
    for more in far[1:]:
        distant = distant + more
    return jnp.where(f - anchor[f] >= 2, distant, earlier(anchor, own, prev))


def distant_pair(far):
    return [far[0][0], *[x[...] for x in far[1:2]]], [far[0][1], *[x[...] for x in far[2:3]]]


def near_kernel(anchor, q, k, v, prev, part, stats, keys, values):
    rows = q.shape[0]
    keys[:rows, :] = earlier(anchor, k, prev[0])
    keys[rows:, :] = k[...]
    values[:rows, :] = earlier(anchor, v, prev[1])
    values[rows:, :] = v[...]
    for c in range(rows // Q_CHUNK):
        at = pl.ds(c * Q_CHUNK, Q_CHUNK)
        scores = dot(keys[...], q[at, :], ((1,), (1,)))
        highest = jnp.max(scores, axis=0, keepdims=True)
        raw = jnp.exp2((scores - highest) * SCALE_LOG2)
        part[0, :, at] = dot(values[...], raw.astype(BF16), ((0,), (0,)))
        stats[0, 0:1, at] = highest
        stats[0, 1:2, at] = jnp.sum(raw, axis=0, keepdims=True)


def far_kernel(count, anchor, q, k, v, prev, *rest):
    far_k, far_v = distant_pair(rest[:count])
    part, near, grad, *columns = rest[count : count + 7]
    out, stats, keep, send, pieces, turned = rest[count + 7 :]
    rows = q.shape[0]
    tm = lax.axis_index("tm")
    sel = (tm % 2) * 2 + (tm // 2) % 2

    @pl.when(pl.program_id(0) == 0)
    def _():
        for m, piece in enumerate(columns):
            pieces[m] = piece[...]

    keys = furthest(anchor, k, prev[0], far_k)
    values = furthest(anchor, v, prev[1], far_v)
    for c in range(rows // Q_CHUNK):
        at = pl.ds(c * Q_CHUNK, Q_CHUNK)
        scores = dot(keys, q[at, :], ((1,), (1,)))
        before = near[0, 0:1, at]
        highest = jnp.maximum(jnp.max(scores, axis=0, keepdims=True), before)
        raw = jnp.exp2((scores - highest) * SCALE_LOG2)
        fade = jnp.exp2((before - highest) * SCALE_LOG2)
        total = jnp.sum(raw, axis=0, keepdims=True) + near[0, 1:2, at] * fade
        attended = dot(values, raw.astype(BF16), ((0,), (0,))) + part[0, :, at] * fade
        attended = attended / total
        turned[:, at] = attended.astype(BF16)
        out[at, :] = attended.T.astype(BF16)
        delta = jnp.sum(attended * grad[at, :].astype(F32).T, axis=0, keepdims=True)
        stats[0, 0:1, at] = highest * SCALE_LOG2 + jnp.log2(total)
        stats[0, 1:2, at] = delta
    for at, slot in enumerate((1, 3)):
        send[at] = dot(turned[...], pieces[slot ^ sel], ((1,), (0,))).astype(BF16)
    for at, slot in enumerate((0, 2)):
        keep[at] = dot(turned[...], pieces[slot ^ sel], ((1,), (0,)))


def backward_kernel(count, lower, anchor, q, k, v, prev, *rest):
    far_k, far_v = distant_pair(rest[:count])
    grad, stats, dq, own_grad, near_dk, near_dv, stays, leaves = rest[count : count + 8]
    keys, values, dk, dv = rest[count + 8 :]
    rows = q.shape[0]
    keys[:rows, :] = furthest(anchor, k, prev[0], far_k)
    keys[rows : 2 * rows, :] = earlier(anchor, k, prev[0])
    keys[2 * rows :, :] = k[...]
    values[:rows, :] = furthest(anchor, v, prev[1], far_v)
    values[rows : 2 * rows, :] = earlier(anchor, v, prev[1])
    values[2 * rows :, :] = v[...]
    for c in range(rows // Q_CHUNK):
        at = pl.ds(c * Q_CHUNK, Q_CHUNK)
        queries, cot = q[at, :], grad[at, :]
        scores = dot(keys[...], queries, ((1,), (1,)))
        prob = jnp.exp2(scores * SCALE_LOG2 - stats[0, 0:1, at])
        prob_grad = dot(values[...], cot, ((1,), (1,)))
        score_grad = (prob * (prob_grad - stats[0, 1:2, at])).astype(BF16)
        dv_term = dot(prob.astype(BF16), cot, ((1,), (0,)))
        dk_term = dot(score_grad, queries, ((1,), (0,)))
        if c == 0:
            dv[...] = dv_term
            dk[...] = dk_term
        else:
            dv[...] += dv_term
            dk[...] += dk_term
        dq_t = dot(keys[...], score_grad, ((0,), (0,))) * SCALE
        dq[at, :] = dq_t.T.astype(BF16)
    f = lax.axis_index("tm")
    a = anchor[f]
    distant = []
    for kind, (ref, near, factor) in enumerate(((dk, near_dk, SCALE), (dv, near_dv, None))):
        parts = [ref[pl.ds(block * rows, rows), :] for block in range(3)]
        if factor is not None:
            parts = [part * factor for part in parts]
        close = parts[1] + jnp.where(f - a >= 2, 0.0, parts[0])
        distant.append(jnp.where(f - a >= 2, parts[0], 0.0).astype(BF16))
        near[...] = jnp.where(a < f, close, 0.0).astype(BF16)
        own_grad[kind] = parts[2] + jnp.where(a < f, 0.0, close)
    swapped = f != lower
    stays[...] = jnp.where(swapped, distant[1], distant[0])
    leaves[...] = jnp.where(swapped, distant[0], distant[1])


def output_kernel(attended, weight, keep, send):
    head = lax.axis_index("head")
    width = weight.shape[0]
    for m in range(4):
        start = pl.multiple_of((head ^ m) * width, 128)
        part = dot(attended[...], weight[:, pl.ds(start, width)], ((1,), (0,)))
        if m % 2:
            send[m // 2] = part.astype(BF16)
        else:
            keep[m // 2] = part


def assemble_kernel(own, other, last, out):
    head = lax.axis_index("head")
    tm = lax.axis_index("tm")
    sel = (tm % 2) * 2 + (tm // 2) % 2
    width = own.shape[0]
    for slot, value in enumerate((own[...], last[0], other[...], last[1])):
        start = pl.multiple_of((head ^ sel ^ slot) * width, 128)
        out[:, pl.ds(start, width)] = value.astype(out.dtype)


def swap(array, axis, bit):
    return lax.ppermute(array, axis, [(i, i ^ bit) for i in range(lax.axis_size(axis))])


def local(query_rows, key_rows, value_rows, output_weight, output_grad, anchor):
    rows, cols = query_rows.shape
    heads = cols // HEAD_DIM
    frames = lax.axis_size("tm")
    seg = min(8, frames // 2)
    bounds = anchor_bounds(frames, seg)
    near_pairs = [(f - 1, f) for f in range(1, frames) if bounds[f][0] < f]
    far_frames = [f for f in range(frames) if f - bounds[f][0] >= 2]
    pair_plan = len(far_frames) == 2 and all(bounds[f][0] == bounds[f][1] for f in far_frames)

    def send(array, pairs):
        return lax.ppermute(array, "tm", pairs)

    def back(pairs):
        return [(b, a) for a, b in pairs]

    own_pair = jnp.stack([key_rows, value_rows])
    prev = send(own_pair, near_pairs)
    if pair_plan:
        lower, upper = far_frames
        source = bounds[lower][0]
        far = (
            send(own_pair, [(source, lower)]),
            send(key_rows, [(source, upper)]),
            send(prev[1], [(source + 1, upper)]),
        )
    else:
        position = lax.axis_index("tm")
        own_anchor = jnp.sum(jnp.where(jnp.arange(frames) == position, anchor, 0))
        distance = position - own_anchor
        fetched = jnp.where(distance == 0, own_pair, prev)
        step = 2
        while step < seg:
            pairs = [(f - step, f) for f in range(step, frames) if f - bounds[f][0] >= step]
            fetched = jnp.where(distance >= step, send(fetched, pairs), fetched)
            step *= 2
        far = (fetched,)

    columns = (output_grad, *[swap(output_grad, "head", m) for m in (1, 2, 3)])
    attended_grad = pl.pallas_call(
        cotangent_kernel,
        out_shape=jax.ShapeDtypeStruct((rows, cols), BF16),
        in_specs=[vmem()] * 5,
        out_specs=vmem(),
        compiler_params=params(8),
        name="cotangent",
    )(*columns, output_weight)

    by_head = pl.BlockSpec((rows, HEAD_DIM), lambda h: (0, h))
    pair_by_head = pl.BlockSpec((2, rows, HEAD_DIM), lambda h: (0, 0, h))
    stat_spec = pl.BlockSpec((1, 8, rows), lambda h: (h, 0, 0))
    part_spec = pl.BlockSpec((1, HEAD_DIM, rows), lambda h: (h, 0, 0))
    narrow = jax.ShapeDtypeStruct((rows, cols), BF16)
    part_shape = jax.ShapeDtypeStruct((heads, HEAD_DIM, rows), F32)
    stat_shape = jax.ShapeDtypeStruct((heads, 8, rows), F32)

    count = len(far)
    near_args = (anchor, query_rows, key_rows, value_rows, prev)
    near_specs = [smem(), by_head, by_head, by_head, pair_by_head]
    far_specs = [*near_specs, pair_by_head, *[by_head] * (count - 1)]
    part, near = pl.pallas_call(
        near_kernel,
        grid=(heads,),
        out_shape=(part_shape, stat_shape),
        in_specs=near_specs,
        out_specs=(part_spec, stat_spec),
        scratch_shapes=[pltpu.VMEM((2 * rows, HEAD_DIM), BF16)] * 2,
        compiler_params=params(12),
        name="near",
    )(*near_args)

    half_spec = pl.BlockSpec((2, HEAD_DIM, cols), lambda h: (0, h, 0))
    attended, stats, keep, away = pl.pallas_call(
        functools.partial(far_kernel, count),
        grid=(heads,),
        out_shape=(
            narrow,
            stat_shape,
            jax.ShapeDtypeStruct((2, cols, cols), F32),
            jax.ShapeDtypeStruct((2, cols, cols), BF16),
        ),
        in_specs=[*far_specs, part_spec, stat_spec, by_head, *[vmem()] * 4],
        out_specs=(by_head, stat_spec, half_spec, half_spec),
        scratch_shapes=[pltpu.VMEM((4, rows, cols), BF16), pltpu.VMEM((HEAD_DIM, rows), BF16)],
        compiler_params=params(14),
        name="far",
    )(*near_args, *far, part, near, attended_grad, *columns)

    query_grad, own_grad, near_dk, near_dv, far_dv, far_dk = pl.pallas_call(
        functools.partial(backward_kernel, count, far_frames[0] if pair_plan else -1),
        grid=(heads,),
        out_shape=(narrow, jax.ShapeDtypeStruct((2, rows, cols), F32), narrow, narrow, narrow, narrow),
        in_specs=[*far_specs, by_head, stat_spec],
        out_specs=(by_head, pair_by_head, *[by_head] * 4),
        scratch_shapes=[pltpu.VMEM((3 * rows, HEAD_DIM), BF16)] * 2
        + [pltpu.VMEM((3 * rows, HEAD_DIM), F32)] * 2,
        compiler_params=params(16),
        name="backward",
    )(*near_args, *far, attended_grad, stats)

    if pair_plan:
        stays, leaves = far_dv, far_dk
        from_k = send(near_dk, back(near_pairs))
        crossing = send(leaves, [(lower, upper), (upper, lower)])
        merged = (stays.astype(F32) + crossing.astype(F32)).astype(BF16)
    if frames == 8:
        arrived, query_grad = lax.optimization_barrier((swap(away, "tm", 2), query_grad))
        half = keep + arrived.astype(F32)
        quarter = (half[0] + swap(half[1].astype(BF16), "tm", 1).astype(F32)).astype(BF16)
        own = (quarter.astype(F32) + swap(quarter, "tm", 4).astype(F32)).astype(BF16)
        own, merged = lax.optimization_barrier((own, merged))
        other = swap(own, "tm", 1)
        sums = (own, other, swap(jnp.stack([own, other]), "tm", 2))
    else:
        sums = (keep[0], keep[1], away.astype(F32))
    weight_grad = pl.pallas_call(
        assemble_kernel,
        out_shape=jax.ShapeDtypeStruct((cols, 4 * cols), F32),
        in_specs=[vmem()] * 3,
        out_specs=vmem(),
        compiler_params=params(8),
        name="assemble",
    )(*sums)
    if frames != 8:
        weight_grad = lax.psum(weight_grad, "tm")

    if pair_plan:
        home_k = send(merged, [(lower, source)]).astype(F32)
        home_v = send(merged, [(upper, source + 1)]).astype(F32)
        from_v = send((near_dv.astype(F32) + home_v).astype(BF16), back(near_pairs)).astype(F32)
        key_total = own_grad[0] + from_k.astype(F32) + home_k
        value_total = own_grad[1] + from_v
    else:
        both = []
        for own, near, far in ((own_grad[0], near_dk, far_dk), (own_grad[1], near_dv, far_dv)):
            held = far.astype(F32)
            step = 2
            while 2 * step < seg:
                step *= 2
            while step >= 2:
                pairs = [(f, f - step) for f in range(step, frames) if f - bounds[f][0] >= step]
                leaving = jnp.where(distance >= step, held, 0.0)
                held = (held - leaving) + send(leaving.astype(BF16), pairs).astype(F32)
                step //= 2
            to_prev = near.astype(F32) + jnp.where(distance == 1, held, 0.0)
            from_near = send(to_prev.astype(BF16), back(near_pairs)).astype(F32)
            both.append(own + from_near + jnp.where(distance == 0, held, 0.0))
        key_total, value_total = both
    key_grad, value_grad = key_total.astype(BF16), value_total.astype(BF16)

    out_keep, out_send = pl.pallas_call(
        output_kernel,
        out_shape=(
            jax.ShapeDtypeStruct((2, rows, cols), F32),
            jax.ShapeDtypeStruct((2, rows, cols), BF16),
        ),
        in_specs=[vmem()] * 2,
        out_specs=(vmem(), vmem()),
        compiler_params=params(8),
        name="output",
    )(attended, output_weight)
    pair_sum = out_keep + swap(out_send, "head", 1).astype(F32)
    layer_output = (pair_sum[0] + swap(pair_sum[1].astype(BF16), "head", 2).astype(F32)).astype(BF16)
    return layer_output, query_grad, key_grad, value_grad, weight_grad


def solution(mesh):
    in_specs = (
        P("tm", "head"),
        P("tm", "head"),
        P("tm", "head"),
        P("head", None),
        P("tm", "head"),
        P(),
    )
    out_specs = (
        P("tm", "head"),
        P("tm", "head"),
        P("tm", "head"),
        P("tm", "head"),
        P("head", None),
    )
    return jax.shard_map(local, mesh=mesh, in_specs=in_specs, out_specs=out_specs, check_vma=False)
```

```python
import functools
import math

import jax
import jax.numpy as jnp
from jax import lax
from jax.experimental import pallas as pl
from jax.experimental.pallas import tpu as pltpu
from jax.sharding import PartitionSpec as P

HEAD_DIM = 128
BF16 = jnp.bfloat16
F32 = jnp.float32
SCALE = HEAD_DIM ** -0.5
SCALE_LOG2 = SCALE * math.log2(math.e)
Q_CHUNK = 256


def dot(a, b, dims):
    return lax.dot_general(a, b, (dims, ((), ())), preferred_element_type=F32)


def anchor_bounds(frames, seg):
    forced = frames // 2 - 2
    bounds = []
    for f in range(frames):
        if f < forced:
            bounds.append((max(0, f - seg + 1), f))
        elif f < forced + seg:
            bounds.append((forced, forced))
        else:
            bounds.append((max(forced + seg, f - seg + 1), f))
    return bounds


def vmem():
    return pl.BlockSpec(memory_space=pltpu.VMEM)


def smem():
    return pl.BlockSpec(memory_space=pltpu.SMEM)


def params(mebibytes):
    return pltpu.CompilerParams(vmem_limit_bytes=mebibytes * 1024 * 1024)


def cotangent_kernel(own, second, third, fourth, weight, out):
    head = lax.axis_index("head")
    width = own.shape[1]
    total = None
    for m, piece in enumerate((own, second, third, fourth)):
        start = pl.multiple_of((head ^ m) * width, 128)
        term = dot(piece[...], weight[:, pl.ds(start, width)], ((1,), (1,)))
        total = term if total is None else total + term
    out[...] = total.astype(BF16)


def earlier(anchor, own, prev):
    f = lax.axis_index("tm")
    return jnp.where(anchor[f] < f, prev, own[...])


def furthest(anchor, own, prev, far):
    f = lax.axis_index("tm")
    distant = far[0]
    for more in far[1:]:
        distant = distant + more
    return jnp.where(f - anchor[f] >= 2, distant, earlier(anchor, own, prev))


def distant_pair(far):
    return [far[0][0], *[x[...] for x in far[1:2]]], [far[0][1], *[x[...] for x in far[2:3]]]


def near_kernel(anchor, q, k, v, prev, part, stats, keys, values):
    rows = q.shape[0]
    keys[:rows, :] = earlier(anchor, k, prev[0])
    keys[rows:, :] = k[...]
    values[:rows, :] = earlier(anchor, v, prev[1])
    values[rows:, :] = v[...]
    for c in range(rows // Q_CHUNK):
        at = pl.ds(c * Q_CHUNK, Q_CHUNK)
        scores = dot(keys[...], q[at, :], ((1,), (1,)))
        highest = jnp.max(scores, axis=0, keepdims=True)
        raw = jnp.exp2((scores - highest) * SCALE_LOG2)
        part[0, :, at] = dot(values[...], raw.astype(BF16), ((0,), (0,)))
        stats[0, 0:1, at] = highest
        stats[0, 1:2, at] = jnp.sum(raw, axis=0, keepdims=True)


def far_kernel(count, anchor, q, k, v, prev, *rest):
    far_k, far_v = distant_pair(rest[:count])
    part, near, grad, *columns = rest[count : count + 7]
    out, stats, keep, send, pieces, turned = rest[count + 7 :]
    rows = q.shape[0]
    tm = lax.axis_index("tm")
    sel = (tm % 2) * 2 + (tm // 2) % 2

    @pl.when(pl.program_id(0) == 0)
    def _():
        for m, piece in enumerate(columns):
            pieces[m] = piece[...]

    keys = furthest(anchor, k, prev[0], far_k)
    values = furthest(anchor, v, prev[1], far_v)
    for c in range(rows // Q_CHUNK):
        at = pl.ds(c * Q_CHUNK, Q_CHUNK)
        scores = dot(keys, q[at, :], ((1,), (1,)))
        before = near[0, 0:1, at]
        highest = jnp.maximum(jnp.max(scores, axis=0, keepdims=True), before)
        raw = jnp.exp2((scores - highest) * SCALE_LOG2)
        fade = jnp.exp2((before - highest) * SCALE_LOG2)
        total = jnp.sum(raw, axis=0, keepdims=True) + near[0, 1:2, at] * fade
        attended = dot(values, raw.astype(BF16), ((0,), (0,))) + part[0, :, at] * fade
        attended = attended / total
        turned[:, at] = attended.astype(BF16)
        out[at, :] = attended.T.astype(BF16)
        delta = jnp.sum(attended * grad[at, :].astype(F32).T, axis=0, keepdims=True)
        stats[0, 0:1, at] = highest * SCALE_LOG2 + jnp.log2(total)
        stats[0, 1:2, at] = delta
    def term(slot):
        return dot(turned[...], pieces[slot ^ sel], ((1,), (0,)))

    row = pl.program_id(0) * HEAD_DIM + lax.broadcasted_iota(jnp.int32, keep.shape[1:], 0)
    upper = row < keep.shape[2] // 2
    second, third = term(1), term(2)
    send[0] = jnp.where(upper, third, second).astype(BF16)
    send[1] = term(3).astype(BF16)
    keep[0] = term(0)
    keep[1] = jnp.where(upper, second, third)


def backward_kernel(count, lower, anchor, q, k, v, prev, *rest):
    far_k, far_v = distant_pair(rest[:count])
    grad, stats, dq, own_grad, near_dk, near_dv, stays, leaves = rest[count : count + 8]
    keys, values, dk, dv = rest[count + 8 :]
    rows = q.shape[0]
    keys[:rows, :] = furthest(anchor, k, prev[0], far_k)
    keys[rows : 2 * rows, :] = earlier(anchor, k, prev[0])
    keys[2 * rows :, :] = k[...]
    values[:rows, :] = furthest(anchor, v, prev[1], far_v)
    values[rows : 2 * rows, :] = earlier(anchor, v, prev[1])
    values[2 * rows :, :] = v[...]
    for c in range(rows // Q_CHUNK):
        at = pl.ds(c * Q_CHUNK, Q_CHUNK)
        queries, cot = q[at, :], grad[at, :]
        scores = dot(keys[...], queries, ((1,), (1,)))
        prob = jnp.exp2(scores * SCALE_LOG2 - stats[0, 0:1, at])
        prob_grad = dot(values[...], cot, ((1,), (1,)))
        score_grad = (prob * (prob_grad - stats[0, 1:2, at])).astype(BF16)
        dv_term = dot(prob.astype(BF16), cot, ((1,), (0,)))
        dk_term = dot(score_grad, queries, ((1,), (0,)))
        if c == 0:
            dv[...] = dv_term
            dk[...] = dk_term
        else:
            dv[...] += dv_term
            dk[...] += dk_term
        dq_t = dot(keys[...], score_grad, ((0,), (0,))) * SCALE
        dq[at, :] = dq_t.T.astype(BF16)
    f = lax.axis_index("tm")
    a = anchor[f]
    distant = []
    for kind, (ref, near, factor) in enumerate(((dk, near_dk, SCALE), (dv, near_dv, None))):
        parts = [ref[pl.ds(block * rows, rows), :] for block in range(3)]
        if factor is not None:
            parts = [part * factor for part in parts]
        close = parts[1] + jnp.where(f - a >= 2, 0.0, parts[0])
        distant.append(jnp.where(f - a >= 2, parts[0], 0.0).astype(BF16))
        near[...] = jnp.where(a < f, close, 0.0).astype(BF16)
        own_grad[kind] = parts[2] + jnp.where(a < f, 0.0, close)
    swapped = f != lower
    stays[...] = jnp.where(swapped, distant[1], distant[0])
    leaves[...] = jnp.where(swapped, distant[0], distant[1])


def output_kernel(attended, weight, keep, send):
    head = lax.axis_index("head")
    width = weight.shape[0]
    for m in range(4):
        start = pl.multiple_of((head ^ m) * width, 128)
        part = dot(attended[...], weight[:, pl.ds(start, width)], ((1,), (0,)))
        if m % 2:
            send[m // 2] = part.astype(BF16)
        else:
            keep[m // 2] = part


def assemble_kernel(*refs):
    *parts, out = refs
    head = lax.axis_index("head")
    tm = lax.axis_index("tm")
    sel = (tm % 2) * 2 + (tm // 2) % 2
    row = 0
    for group, (second, others) in enumerate(((1, (2, 3)), (2, (1, 3)))):
        first_ref, second_ref, last_ref = parts[3 * group : 3 * group + 3]
        height, width = first_ref.shape
        values = {0: first_ref[...], second: second_ref[...], others[0]: last_ref[0], others[1]: last_ref[1]}
        for slot, value in values.items():
            start = pl.multiple_of((head ^ sel ^ slot) * width, 128)
            out[row : row + height, pl.ds(start, width)] = value.astype(out.dtype)
        row += height


def swap(array, axis, bit):
    return lax.ppermute(array, axis, [(i, i ^ bit) for i in range(lax.axis_size(axis))])


def local(query_rows, key_rows, value_rows, output_weight, output_grad, anchor):
    rows, cols = query_rows.shape
    heads = cols // HEAD_DIM
    frames = lax.axis_size("tm")
    seg = min(8, frames // 2)
    bounds = anchor_bounds(frames, seg)
    near_pairs = [(f - 1, f) for f in range(1, frames) if bounds[f][0] < f]
    far_frames = [f for f in range(frames) if f - bounds[f][0] >= 2]
    pair_plan = len(far_frames) == 2 and all(bounds[f][0] == bounds[f][1] for f in far_frames)

    def send(array, pairs):
        return lax.ppermute(array, "tm", pairs)

    def back(pairs):
        return [(b, a) for a, b in pairs]

    own_pair = jnp.stack([key_rows, value_rows])
    prev = send(own_pair, near_pairs)
    if pair_plan:
        lower, upper = far_frames
        source = bounds[lower][0]
        far = (
            send(own_pair, [(source, lower)]),
            send(key_rows, [(source, upper)]),
            send(prev[1], [(source + 1, upper)]),
        )
    else:
        position = lax.axis_index("tm")
        own_anchor = jnp.sum(jnp.where(jnp.arange(frames) == position, anchor, 0))
        distance = position - own_anchor
        fetched = jnp.where(distance == 0, own_pair, prev)
        step = 2
        while step < seg:
            pairs = [(f - step, f) for f in range(step, frames) if f - bounds[f][0] >= step]
            fetched = jnp.where(distance >= step, send(fetched, pairs), fetched)
            step *= 2
        far = (fetched,)

    columns = (output_grad, *[swap(output_grad, "head", m) for m in (1, 2, 3)])
    attended_grad = pl.pallas_call(
        cotangent_kernel,
        out_shape=jax.ShapeDtypeStruct((rows, cols), BF16),
        in_specs=[vmem()] * 5,
        out_specs=vmem(),
        compiler_params=params(8),
        name="cotangent",
    )(*columns, output_weight)

    by_head = pl.BlockSpec((rows, HEAD_DIM), lambda h: (0, h))
    pair_by_head = pl.BlockSpec((2, rows, HEAD_DIM), lambda h: (0, 0, h))
    stat_spec = pl.BlockSpec((1, 8, rows), lambda h: (h, 0, 0))
    part_spec = pl.BlockSpec((1, HEAD_DIM, rows), lambda h: (h, 0, 0))
    narrow = jax.ShapeDtypeStruct((rows, cols), BF16)
    part_shape = jax.ShapeDtypeStruct((heads, HEAD_DIM, rows), F32)
    stat_shape = jax.ShapeDtypeStruct((heads, 8, rows), F32)

    count = len(far)
    near_args = (anchor, query_rows, key_rows, value_rows, prev)
    near_specs = [smem(), by_head, by_head, by_head, pair_by_head]
    far_specs = [*near_specs, pair_by_head, *[by_head] * (count - 1)]
    part, near = pl.pallas_call(
        near_kernel,
        grid=(heads,),
        out_shape=(part_shape, stat_shape),
        in_specs=near_specs,
        out_specs=(part_spec, stat_spec),
        scratch_shapes=[pltpu.VMEM((2 * rows, HEAD_DIM), BF16)] * 2,
        compiler_params=params(12),
        name="near",
    )(*near_args)

    half_spec = pl.BlockSpec((2, HEAD_DIM, cols), lambda h: (0, h, 0))
    attended, stats, keep, away = pl.pallas_call(
        functools.partial(far_kernel, count),
        grid=(heads,),
        out_shape=(
            narrow,
            stat_shape,
            jax.ShapeDtypeStruct((2, cols, cols), F32),
            jax.ShapeDtypeStruct((2, cols, cols), BF16),
        ),
        in_specs=[*far_specs, part_spec, stat_spec, by_head, *[vmem()] * 4],
        out_specs=(by_head, stat_spec, half_spec, half_spec),
        scratch_shapes=[pltpu.VMEM((4, rows, cols), BF16), pltpu.VMEM((HEAD_DIM, rows), BF16)],
        compiler_params=params(14),
        name="far",
    )(*near_args, *far, part, near, attended_grad, *columns)

    query_grad, own_grad, near_dk, near_dv, far_dv, far_dk = pl.pallas_call(
        functools.partial(backward_kernel, count, far_frames[0] if pair_plan else -1),
        grid=(heads,),
        out_shape=(narrow, jax.ShapeDtypeStruct((2, rows, cols), F32), narrow, narrow, narrow, narrow),
        in_specs=[*far_specs, by_head, stat_spec],
        out_specs=(by_head, pair_by_head, *[by_head] * 4),
        scratch_shapes=[pltpu.VMEM((3 * rows, HEAD_DIM), BF16)] * 2
        + [pltpu.VMEM((3 * rows, HEAD_DIM), F32)] * 2,
        compiler_params=params(16),
        name="backward",
    )(*near_args, *far, attended_grad, stats)

    if pair_plan:
        stays, leaves = far_dv, far_dk
        from_k = send(near_dk, back(near_pairs))
    keep_a, keep_b = keep[:, : cols // 2], keep[:, cols // 2 :]
    away_a, away_b = away[:, : cols // 2], away[:, cols // 2 :]
    if frames == 8:
        arrived_a, arrived_b = swap(away_a, "tm", 1), swap(away_b, "tm", 2)
        arrived_a, arrived_b, query_grad = lax.optimization_barrier((arrived_a, arrived_b, query_grad))
        half_a, half_b = keep_a + arrived_a.astype(F32), keep_b + arrived_b.astype(F32)
        quarter_a = half_a[0] + swap(half_a[1].astype(BF16), "tm", 2).astype(F32)
        quarter_b = half_b[0] + swap(half_b[1].astype(BF16), "tm", 1).astype(F32)
        quarter = jnp.concatenate([quarter_a, quarter_b], 0).astype(BF16)
        quarter, leaves = lax.optimization_barrier((quarter, leaves))
        crossing = send(leaves, [(lower, upper), (upper, lower)])
        merged = (stays.astype(F32) + crossing.astype(F32)).astype(BF16)
        own = (quarter.astype(F32) + swap(quarter, "tm", 4).astype(F32)).astype(BF16)
        own, merged = lax.optimization_barrier((own, merged))
        own_a, own_b = own[: cols // 2], own[cols // 2 :]
        other_a, other_b = swap(own_a, "tm", 2), swap(own_b, "tm", 1)
        sums = (
            *(own_a, other_a, swap(jnp.stack([own_a, other_a]), "tm", 1)),
            *(own_b, other_b, swap(jnp.stack([own_b, other_b]), "tm", 2)),
        )
    else:
        sums = (keep_a[0], keep_a[1], away_a.astype(F32), keep_b[0], keep_b[1], away_b.astype(F32))
    weight_grad = pl.pallas_call(
        assemble_kernel,
        out_shape=jax.ShapeDtypeStruct((cols, 4 * cols), F32),
        in_specs=[vmem()] * 6,
        out_specs=vmem(),
        compiler_params=params(8),
        name="assemble",
    )(*sums)
    if frames != 8:
        weight_grad = lax.psum(weight_grad, "tm")

    if pair_plan:
        home_k = send(merged, [(lower, source)]).astype(F32)
        home_v = send(merged, [(upper, source + 1)])
        if frames == 8:
            home_v = lax.optimization_barrier((home_v, other_a, other_b))[0]
        from_v = send((near_dv.astype(F32) + home_v.astype(F32)).astype(BF16), back(near_pairs)).astype(F32)
        key_total = own_grad[0] + from_k.astype(F32) + home_k
        value_total = own_grad[1] + from_v
    else:
        both = []
        for own, near, far in ((own_grad[0], near_dk, far_dk), (own_grad[1], near_dv, far_dv)):
            held = far.astype(F32)
            step = 2
            while 2 * step < seg:
                step *= 2
            while step >= 2:
                pairs = [(f, f - step) for f in range(step, frames) if f - bounds[f][0] >= step]
                leaving = jnp.where(distance >= step, held, 0.0)
                held = (held - leaving) + send(leaving.astype(BF16), pairs).astype(F32)
                step //= 2
            to_prev = near.astype(F32) + jnp.where(distance == 1, held, 0.0)
            from_near = send(to_prev.astype(BF16), back(near_pairs)).astype(F32)
            both.append(own + from_near + jnp.where(distance == 0, held, 0.0))
        key_total, value_total = both
    key_grad, value_grad = key_total.astype(BF16), value_total.astype(BF16)

    out_keep, out_send = pl.pallas_call(
        output_kernel,
        out_shape=(
            jax.ShapeDtypeStruct((2, rows, cols), F32),
            jax.ShapeDtypeStruct((2, rows, cols), BF16),
        ),
        in_specs=[vmem()] * 2,
        out_specs=(vmem(), vmem()),
        compiler_params=params(8),
        name="output",
    )(attended, output_weight)
    pair_sum = out_keep + swap(out_send, "head", 1).astype(F32)
    layer_output = (pair_sum[0] + swap(pair_sum[1].astype(BF16), "head", 2).astype(F32)).astype(BF16)
    return layer_output, query_grad, key_grad, value_grad, weight_grad


def solution(mesh):
    in_specs = (
        P("tm", "head"),
        P("tm", "head"),
        P("tm", "head"),
        P("head", None),
        P("tm", "head"),
        P(),
    )
    out_specs = (
        P("tm", "head"),
        P("tm", "head"),
        P("tm", "head"),
        P("tm", "head"),
        P("head", None),
    )
    return jax.shard_map(local, mesh=mesh, in_specs=in_specs, out_specs=out_specs, check_vma=False)
```

```python
import functools
import math

import jax
import jax.numpy as jnp
from jax import lax
from jax.experimental import pallas as pl
from jax.experimental.pallas import tpu as pltpu
from jax.sharding import PartitionSpec as P

HEAD_DIM = 128
BF16 = jnp.bfloat16
F32 = jnp.float32
SCALE = HEAD_DIM ** -0.5
SCALE_LOG2 = SCALE * math.log2(math.e)
Q_CHUNK = 256


def dot(a, b, dims):
    return lax.dot_general(a, b, (dims, ((), ())), preferred_element_type=F32)


def anchor_bounds(frames, seg):
    forced = frames // 2 - 2
    bounds = []
    for f in range(frames):
        if f < forced:
            bounds.append((max(0, f - seg + 1), f))
        elif f < forced + seg:
            bounds.append((forced, forced))
        else:
            bounds.append((max(forced + seg, f - seg + 1), f))
    return bounds


def vmem():
    return pl.BlockSpec(memory_space=pltpu.VMEM)


def smem():
    return pl.BlockSpec(memory_space=pltpu.SMEM)


def params(mebibytes):
    return pltpu.CompilerParams(vmem_limit_bytes=mebibytes * 1024 * 1024)


def cotangent_kernel(own, second, third, fourth, weight, out):
    head = lax.axis_index("head")
    width = own.shape[1]
    total = None
    for m, piece in enumerate((own, second, third, fourth)):
        start = pl.multiple_of((head ^ m) * width, 128)
        term = dot(piece[...], weight[:, pl.ds(start, width)], ((1,), (1,)))
        total = term if total is None else total + term
    out[...] = total.astype(BF16)


def earlier(anchor, own, prev):
    f = lax.axis_index("tm")
    return jnp.where(anchor[f] < f, prev, own[...])


def furthest(anchor, own, prev, far):
    f = lax.axis_index("tm")
    distant = far[0]
    for more in far[1:]:
        distant = distant + more
    return jnp.where(f - anchor[f] >= 2, distant, earlier(anchor, own, prev))


def distant_pair(far):
    return [far[0][0], *[x[...] for x in far[1:2]]], [far[0][1], *[x[...] for x in far[2:3]]]


def near_kernel(anchor, q, k, v, prev, part, stats, keys, values):
    rows = q.shape[0]
    keys[:rows, :] = earlier(anchor, k, prev[0])
    keys[rows:, :] = k[...]
    values[:rows, :] = earlier(anchor, v, prev[1])
    values[rows:, :] = v[...]
    for c in range(rows // Q_CHUNK):
        at = pl.ds(c * Q_CHUNK, Q_CHUNK)
        scores = dot(keys[...], q[at, :], ((1,), (1,)))
        highest = jnp.max(scores, axis=0, keepdims=True)
        raw = jnp.exp2((scores - highest) * SCALE_LOG2)
        part[0, :, at] = dot(values[...], raw.astype(BF16), ((0,), (0,)))
        stats[0, 0:1, at] = highest
        stats[0, 1:2, at] = jnp.sum(raw, axis=0, keepdims=True)


def far_kernel(count, anchor, q, k, v, prev, *rest):
    far_k, far_v = distant_pair(rest[:count])
    part, near, grad, *columns = rest[count : count + 7]
    out, stats, keep, send, pieces, turned = rest[count + 7 :]
    rows = q.shape[0]
    tm = lax.axis_index("tm")
    sel = (tm % 2) * 2 + (tm // 2) % 2

    @pl.when(pl.program_id(0) == 0)
    def _():
        for m, piece in enumerate(columns):
            pieces[m] = piece[...]

    keys = furthest(anchor, k, prev[0], far_k)
    values = furthest(anchor, v, prev[1], far_v)
    for c in range(rows // Q_CHUNK):
        at = pl.ds(c * Q_CHUNK, Q_CHUNK)
        scores = dot(keys, q[at, :], ((1,), (1,)))
        before = near[0, 0:1, at]
        highest = jnp.maximum(jnp.max(scores, axis=0, keepdims=True), before)
        raw = jnp.exp2((scores - highest) * SCALE_LOG2)
        fade = jnp.exp2((before - highest) * SCALE_LOG2)
        total = jnp.sum(raw, axis=0, keepdims=True) + near[0, 1:2, at] * fade
        attended = dot(values, raw.astype(BF16), ((0,), (0,))) + part[0, :, at] * fade
        attended = attended / total
        turned[:, at] = attended.astype(BF16)
        out[at, :] = attended.T.astype(BF16)
        delta = jnp.sum(attended * grad[at, :].astype(F32).T, axis=0, keepdims=True)
        stats[0, 0:1, at] = highest * SCALE_LOG2 + jnp.log2(total)
        stats[0, 1:2, at] = delta
    def term(slot):
        return dot(turned[...], pieces[slot ^ sel], ((1,), (0,)))

    row = pl.program_id(0) * HEAD_DIM + lax.broadcasted_iota(jnp.int32, keep.shape[1:], 0)
    upper = row < keep.shape[2] // 2
    second, third = term(1), term(2)
    send[0] = jnp.where(upper, third, second).astype(BF16)
    send[1] = term(3).astype(BF16)
    keep[0] = term(0)
    keep[1] = jnp.where(upper, second, third)


def backward_kernel(count, lower, anchor, q, k, v, prev, *rest):
    far_k, far_v = distant_pair(rest[:count])
    grad, stats, dq, own_grad, near_dk, near_dv, stays, leaves = rest[count : count + 8]
    keys, values, dk, dv = rest[count + 8 :]
    rows = q.shape[0]
    keys[:rows, :] = furthest(anchor, k, prev[0], far_k)
    keys[rows : 2 * rows, :] = earlier(anchor, k, prev[0])
    keys[2 * rows :, :] = k[...]
    values[:rows, :] = furthest(anchor, v, prev[1], far_v)
    values[rows : 2 * rows, :] = earlier(anchor, v, prev[1])
    values[2 * rows :, :] = v[...]
    for c in range(rows // Q_CHUNK):
        at = pl.ds(c * Q_CHUNK, Q_CHUNK)
        queries, cot = q[at, :], grad[at, :]
        scores = dot(keys[...], queries, ((1,), (1,)))
        prob = jnp.exp2(scores * SCALE_LOG2 - stats[0, 0:1, at])
        prob_grad = dot(values[...], cot, ((1,), (1,)))
        score_grad = (prob * (prob_grad - stats[0, 1:2, at])).astype(BF16)
        dv_term = dot(prob.astype(BF16), cot, ((1,), (0,)))
        dk_term = dot(score_grad, queries, ((1,), (0,)))
        if c == 0:
            dv[...] = dv_term
            dk[...] = dk_term
        else:
            dv[...] += dv_term
            dk[...] += dk_term
        dq_t = dot(keys[...], score_grad, ((0,), (0,))) * SCALE
        dq[at, :] = dq_t.T.astype(BF16)
    f = lax.axis_index("tm")
    a = anchor[f]
    distant = []
    for kind, (ref, near, factor) in enumerate(((dk, near_dk, SCALE), (dv, near_dv, None))):
        parts = [ref[pl.ds(block * rows, rows), :] for block in range(3)]
        if factor is not None:
            parts = [part * factor for part in parts]
        close = parts[1] + jnp.where(f - a >= 2, 0.0, parts[0])
        distant.append(jnp.where(f - a >= 2, parts[0], 0.0).astype(BF16))
        near[...] = jnp.where(a < f, close, 0.0).astype(BF16)
        own_grad[kind] = parts[2] + jnp.where(a < f, 0.0, close)
    swapped = f != lower
    stays[...] = jnp.where(swapped, distant[1], distant[0])
    leaves[...] = jnp.where(swapped, distant[0], distant[1])


def output_kernel(attended, weight, keep, send):
    head = lax.axis_index("head")
    width = weight.shape[0]
    for m in range(4):
        start = pl.multiple_of((head ^ m) * width, 128)
        part = dot(attended[...], weight[:, pl.ds(start, width)], ((1,), (0,)))
        if m % 2:
            send[m // 2] = part.astype(BF16)
        else:
            keep[m // 2] = part


def assemble_kernel(*refs):
    *parts, out = refs
    head = lax.axis_index("head")
    tm = lax.axis_index("tm")
    sel = (tm % 2) * 2 + (tm // 2) % 2
    row = 0
    for group, (second, others) in enumerate(((1, (2, 3)), (2, (1, 3)))):
        first_ref, second_ref, last_ref = parts[3 * group : 3 * group + 3]
        height, width = first_ref.shape
        values = {0: first_ref[...], second: second_ref[...], others[0]: last_ref[0], others[1]: last_ref[1]}
        for slot, value in values.items():
            start = pl.multiple_of((head ^ sel ^ slot) * width, 128)
            out[row : row + height, pl.ds(start, width)] = value.astype(out.dtype)
        row += height


def swap(array, axis, bit):
    return lax.ppermute(array, axis, [(i, i ^ bit) for i in range(lax.axis_size(axis))])


def local(query_rows, key_rows, value_rows, output_weight, output_grad, anchor):
    rows, cols = query_rows.shape
    heads = cols // HEAD_DIM
    frames = lax.axis_size("tm")
    seg = min(8, frames // 2)
    bounds = anchor_bounds(frames, seg)
    near_pairs = [(f - 1, f) for f in range(1, frames) if bounds[f][0] < f]
    far_frames = [f for f in range(frames) if f - bounds[f][0] >= 2]
    pair_plan = len(far_frames) == 2 and all(bounds[f][0] == bounds[f][1] for f in far_frames)

    def send(array, pairs):
        return lax.ppermute(array, "tm", pairs)

    def back(pairs):
        return [(b, a) for a, b in pairs]

    own_pair = jnp.stack([key_rows, value_rows])
    prev = send(own_pair, near_pairs)
    if pair_plan:
        lower, upper = far_frames
        source = bounds[lower][0]
        far = (
            send(own_pair, [(source, lower)]),
            send(key_rows, [(source, upper)]),
            send(prev[1], [(source + 1, upper)]),
        )
    else:
        position = lax.axis_index("tm")
        own_anchor = jnp.sum(jnp.where(jnp.arange(frames) == position, anchor, 0))
        distance = position - own_anchor
        fetched = jnp.where(distance == 0, own_pair, prev)
        step = 2
        while step < seg:
            pairs = [(f - step, f) for f in range(step, frames) if f - bounds[f][0] >= step]
            fetched = jnp.where(distance >= step, send(fetched, pairs), fetched)
            step *= 2
        far = (fetched,)

    across = swap(output_grad, "head", 2)
    columns = (output_grad, swap(output_grad, "head", 1), across, swap(across, "head", 1))
    attended_grad = pl.pallas_call(
        cotangent_kernel,
        out_shape=jax.ShapeDtypeStruct((rows, cols), BF16),
        in_specs=[vmem()] * 5,
        out_specs=vmem(),
        compiler_params=params(8),
        name="cotangent",
    )(*columns, output_weight)

    by_head = pl.BlockSpec((rows, HEAD_DIM), lambda h: (0, h))
    pair_by_head = pl.BlockSpec((2, rows, HEAD_DIM), lambda h: (0, 0, h))
    stat_spec = pl.BlockSpec((1, 8, rows), lambda h: (h, 0, 0))
    part_spec = pl.BlockSpec((1, HEAD_DIM, rows), lambda h: (h, 0, 0))
    narrow = jax.ShapeDtypeStruct((rows, cols), BF16)
    part_shape = jax.ShapeDtypeStruct((heads, HEAD_DIM, rows), F32)
    stat_shape = jax.ShapeDtypeStruct((heads, 8, rows), F32)

    count = len(far)
    near_args = (anchor, query_rows, key_rows, value_rows, prev)
    near_specs = [smem(), by_head, by_head, by_head, pair_by_head]
    far_specs = [*near_specs, pair_by_head, *[by_head] * (count - 1)]
    part, near = pl.pallas_call(
        near_kernel,
        grid=(heads,),
        out_shape=(part_shape, stat_shape),
        in_specs=near_specs,
        out_specs=(part_spec, stat_spec),
        scratch_shapes=[pltpu.VMEM((2 * rows, HEAD_DIM), BF16)] * 2,
        compiler_params=params(12),
        name="near",
    )(*near_args)

    half_spec = pl.BlockSpec((2, HEAD_DIM, cols), lambda h: (0, h, 0))
    attended, stats, keep, away = pl.pallas_call(
        functools.partial(far_kernel, count),
        grid=(heads,),
        out_shape=(
            narrow,
            stat_shape,
            jax.ShapeDtypeStruct((2, cols, cols), F32),
            jax.ShapeDtypeStruct((2, cols, cols), BF16),
        ),
        in_specs=[*far_specs, part_spec, stat_spec, by_head, *[vmem()] * 4],
        out_specs=(by_head, stat_spec, half_spec, half_spec),
        scratch_shapes=[pltpu.VMEM((4, rows, cols), BF16), pltpu.VMEM((HEAD_DIM, rows), BF16)],
        compiler_params=params(14),
        name="far",
    )(*near_args, *far, part, near, attended_grad, *columns)

    query_grad, own_grad, near_dk, near_dv, far_dv, far_dk = pl.pallas_call(
        functools.partial(backward_kernel, count, far_frames[0] if pair_plan else -1),
        grid=(heads,),
        out_shape=(narrow, jax.ShapeDtypeStruct((2, rows, cols), F32), narrow, narrow, narrow, narrow),
        in_specs=[*far_specs, by_head, stat_spec],
        out_specs=(by_head, pair_by_head, *[by_head] * 4),
        scratch_shapes=[pltpu.VMEM((3 * rows, HEAD_DIM), BF16)] * 2
        + [pltpu.VMEM((3 * rows, HEAD_DIM), F32)] * 2,
        compiler_params=params(16),
        name="backward",
    )(*near_args, *far, attended_grad, stats)

    if pair_plan:
        stays, leaves = far_dv, far_dk
        from_k = send(near_dk, back(near_pairs))
    keep_a, keep_b = keep[:, : cols // 2], keep[:, cols // 2 :]
    away_a, away_b = away[:, : cols // 2], away[:, cols // 2 :]
    if frames == 8:
        arrived_a, arrived_b = swap(away_a, "tm", 1), swap(away_b, "tm", 2)
        arrived_a, arrived_b, query_grad = lax.optimization_barrier((arrived_a, arrived_b, query_grad))
        half_a, half_b = keep_a + arrived_a.astype(F32), keep_b + arrived_b.astype(F32)
        quarter_a = half_a[0] + swap(half_a[1].astype(BF16), "tm", 2).astype(F32)
        quarter_b = half_b[0] + swap(half_b[1].astype(BF16), "tm", 1).astype(F32)
        quarter = jnp.concatenate([quarter_a, quarter_b], 0).astype(BF16)
        quarter, leaves = lax.optimization_barrier((quarter, leaves))
        crossing = send(leaves, [(lower, upper), (upper, lower)])
        merged = (stays.astype(F32) + crossing.astype(F32)).astype(BF16)
        own = (quarter.astype(F32) + swap(quarter, "tm", 4).astype(F32)).astype(BF16)
        own, merged = lax.optimization_barrier((own, merged))
        own_a, own_b = own[: cols // 2], own[cols // 2 :]
        other_a, other_b = swap(own_a, "tm", 2), swap(own_b, "tm", 1)
        sums = (
            *(own_a, other_a, swap(jnp.stack([own_a, other_a]), "tm", 1)),
            *(own_b, other_b, swap(jnp.stack([own_b, other_b]), "tm", 2)),
        )
    else:
        sums = (keep_a[0], keep_a[1], away_a.astype(F32), keep_b[0], keep_b[1], away_b.astype(F32))
    weight_grad = pl.pallas_call(
        assemble_kernel,
        out_shape=jax.ShapeDtypeStruct((cols, 4 * cols), F32),
        in_specs=[vmem()] * 6,
        out_specs=vmem(),
        compiler_params=params(8),
        name="assemble",
    )(*sums)
    if frames != 8:
        weight_grad = lax.psum(weight_grad, "tm")

    if pair_plan:
        home_k = send(merged, [(lower, source)]).astype(F32)
        home_v = send(merged, [(upper, source + 1)])
        if frames == 8:
            home_v = lax.optimization_barrier((home_v, other_a, other_b))[0]
        from_v = send((near_dv.astype(F32) + home_v.astype(F32)).astype(BF16), back(near_pairs)).astype(F32)
        key_total = own_grad[0] + from_k.astype(F32) + home_k
        value_total = own_grad[1] + from_v
    else:
        both = []
        for own, near, far in ((own_grad[0], near_dk, far_dk), (own_grad[1], near_dv, far_dv)):
            held = far.astype(F32)
            step = 2
            while 2 * step < seg:
                step *= 2
            while step >= 2:
                pairs = [(f, f - step) for f in range(step, frames) if f - bounds[f][0] >= step]
                leaving = jnp.where(distance >= step, held, 0.0)
                held = (held - leaving) + send(leaving.astype(BF16), pairs).astype(F32)
                step //= 2
            to_prev = near.astype(F32) + jnp.where(distance == 1, held, 0.0)
            from_near = send(to_prev.astype(BF16), back(near_pairs)).astype(F32)
            both.append(own + from_near + jnp.where(distance == 0, held, 0.0))
        key_total, value_total = both
    key_grad, value_grad = key_total.astype(BF16), value_total.astype(BF16)

    out_keep, out_send = pl.pallas_call(
        output_kernel,
        out_shape=(
            jax.ShapeDtypeStruct((2, rows, cols), F32),
            jax.ShapeDtypeStruct((2, rows, cols), BF16),
        ),
        in_specs=[vmem()] * 2,
        out_specs=(vmem(), vmem()),
        compiler_params=params(8),
        name="output",
    )(attended, output_weight)
    pair_sum = out_keep + swap(out_send, "head", 1).astype(F32)
    layer_output = (pair_sum[0] + swap(pair_sum[1].astype(BF16), "head", 2).astype(F32)).astype(BF16)
    return layer_output, query_grad, key_grad, value_grad, weight_grad


def solution(mesh):
    in_specs = (
        P("tm", "head"),
        P("tm", "head"),
        P("tm", "head"),
        P("head", None),
        P("tm", "head"),
        P(),
    )
    out_specs = (
        P("tm", "head"),
        P("tm", "head"),
        P("tm", "head"),
        P("tm", "head"),
        P("head", None),
    )
    return jax.shard_map(local, mesh=mesh, in_specs=in_specs, out_specs=out_specs, check_vma=False)
```

```python
import functools
import math

import jax
import jax.numpy as jnp
from jax import lax
from jax.experimental import pallas as pl
from jax.experimental.pallas import tpu as pltpu
from jax.sharding import PartitionSpec as P

HEAD_DIM = 128
BF16 = jnp.bfloat16
F32 = jnp.float32
SCALE = HEAD_DIM ** -0.5
SCALE_LOG2 = SCALE * math.log2(math.e)
Q_CHUNK = 512


def dot(a, b, dims):
    return lax.dot_general(a, b, (dims, ((), ())), preferred_element_type=F32)


def anchor_bounds(frames, seg):
    forced = frames // 2 - 2
    bounds = []
    for f in range(frames):
        if f < forced:
            bounds.append((max(0, f - seg + 1), f))
        elif f < forced + seg:
            bounds.append((forced, forced))
        else:
            bounds.append((max(forced + seg, f - seg + 1), f))
    return bounds


def vmem():
    return pl.BlockSpec(memory_space=pltpu.VMEM)


def smem():
    return pl.BlockSpec(memory_space=pltpu.SMEM)


def params(mebibytes):
    return pltpu.CompilerParams(vmem_limit_bytes=mebibytes * 1024 * 1024)


def cotangent_kernel(own, second, third, fourth, weight, out):
    head = lax.axis_index("head")
    width = own.shape[1]
    total = None
    for m, piece in enumerate((own, second, third, fourth)):
        start = pl.multiple_of((head ^ m) * width, 128)
        term = dot(piece[...], weight[:, pl.ds(start, width)], ((1,), (1,)))
        total = term if total is None else total + term
    out[...] = total.astype(BF16)


def earlier(anchor, own, prev):
    f = lax.axis_index("tm")
    return jnp.where(anchor[f] < f, prev, own[...])


def furthest(anchor, own, prev, far):
    f = lax.axis_index("tm")
    distant = far[0]
    for more in far[1:]:
        distant = distant + more
    return jnp.where(f - anchor[f] >= 2, distant, earlier(anchor, own, prev))


def distant_pair(far):
    return [far[0][0], *[x[...] for x in far[1:2]]], [far[0][1], *[x[...] for x in far[2:3]]]


def near_kernel(anchor, q, k, v, prev, part, stats, keys, values):
    rows = q.shape[0]
    keys[:rows, :] = earlier(anchor, k, prev[0])
    keys[rows:, :] = k[...]
    values[:rows, :] = earlier(anchor, v, prev[1])
    values[rows:, :] = v[...]
    for c in range(rows // Q_CHUNK):
        at = pl.ds(c * Q_CHUNK, Q_CHUNK)
        scores = dot(keys[...], q[at, :], ((1,), (1,)))
        highest = jnp.max(scores, axis=0, keepdims=True)
        raw = jnp.exp2((scores - highest) * SCALE_LOG2)
        part[0, :, at] = dot(values[...], raw.astype(BF16), ((0,), (0,)))
        stats[0, 0:1, at] = highest
        stats[0, 1:2, at] = jnp.sum(raw, axis=0, keepdims=True)


def far_kernel(count, anchor, q, k, v, prev, *rest):
    far_k, far_v = distant_pair(rest[:count])
    part, near, grad, *columns = rest[count : count + 7]
    out, stats, keep, send, pieces, turned = rest[count + 7 :]
    rows = q.shape[0]
    tm = lax.axis_index("tm")
    sel = (tm % 2) * 2 + (tm // 2) % 2

    @pl.when(pl.program_id(0) == 0)
    def _():
        for m, piece in enumerate(columns):
            pieces[m] = piece[...]

    keys = furthest(anchor, k, prev[0], far_k)
    values = furthest(anchor, v, prev[1], far_v)
    for c in range(rows // Q_CHUNK):
        at = pl.ds(c * Q_CHUNK, Q_CHUNK)
        scores = dot(keys, q[at, :], ((1,), (1,)))
        before = near[0, 0:1, at]
        highest = jnp.maximum(jnp.max(scores, axis=0, keepdims=True), before)
        raw = jnp.exp2((scores - highest) * SCALE_LOG2)
        fade = jnp.exp2((before - highest) * SCALE_LOG2)
        total = jnp.sum(raw, axis=0, keepdims=True) + near[0, 1:2, at] * fade
        attended = dot(values, raw.astype(BF16), ((0,), (0,))) + part[0, :, at] * fade
        attended = attended / total
        turned[:, at] = attended.astype(BF16)
        out[at, :] = attended.T.astype(BF16)
        delta = jnp.sum(attended * grad[at, :].astype(F32).T, axis=0, keepdims=True)
        stats[0, 0:1, at] = highest * SCALE_LOG2 + jnp.log2(total)
        stats[0, 1:2, at] = delta
    def term(slot):
        return dot(turned[...], pieces[slot ^ sel], ((1,), (0,)))

    row = pl.program_id(0) * HEAD_DIM + lax.broadcasted_iota(jnp.int32, keep.shape[1:], 0)
    upper = row < keep.shape[2] // 2
    second, third = term(1), term(2)
    send[0] = jnp.where(upper, third, second).astype(BF16)
    send[1] = term(3).astype(BF16)
    keep[0] = term(0)
    keep[1] = jnp.where(upper, second, third)


def backward_kernel(count, lower, anchor, q, k, v, prev, *rest):
    far_k, far_v = distant_pair(rest[:count])
    grad, stats, dq, own_grad, near_dk, near_dv, stays, leaves = rest[count : count + 8]
    keys, values, dk, dv = rest[count + 8 :]
    rows = q.shape[0]
    keys[:rows, :] = furthest(anchor, k, prev[0], far_k)
    keys[rows : 2 * rows, :] = earlier(anchor, k, prev[0])
    keys[2 * rows :, :] = k[...]
    values[:rows, :] = furthest(anchor, v, prev[1], far_v)
    values[rows : 2 * rows, :] = earlier(anchor, v, prev[1])
    values[2 * rows :, :] = v[...]
    for c in range(rows // Q_CHUNK):
        at = pl.ds(c * Q_CHUNK, Q_CHUNK)
        queries, cot = q[at, :], grad[at, :]
        scores = dot(keys[...], queries, ((1,), (1,)))
        prob = jnp.exp2(scores * SCALE_LOG2 - stats[0, 0:1, at])
        prob_grad = dot(values[...], cot, ((1,), (1,)))
        score_grad = (prob * (prob_grad - stats[0, 1:2, at])).astype(BF16)
        dv_term = dot(prob.astype(BF16), cot, ((1,), (0,)))
        dk_term = dot(score_grad, queries, ((1,), (0,)))
        if c == 0:
            dv[...] = dv_term
            dk[...] = dk_term
        else:
            dv[...] += dv_term
            dk[...] += dk_term
        dq_t = dot(keys[...], score_grad, ((0,), (0,))) * SCALE
        dq[at, :] = dq_t.T.astype(BF16)
    f = lax.axis_index("tm")
    a = anchor[f]
    distant = []
    for kind, (ref, near, factor) in enumerate(((dk, near_dk, SCALE), (dv, near_dv, None))):
        parts = [ref[pl.ds(block * rows, rows), :] for block in range(3)]
        if factor is not None:
            parts = [part * factor for part in parts]
        close = parts[1] + jnp.where(f - a >= 2, 0.0, parts[0])
        distant.append(jnp.where(f - a >= 2, parts[0], 0.0).astype(BF16))
        near[...] = jnp.where(a < f, close, 0.0).astype(BF16)
        own_grad[kind] = parts[2] + jnp.where(a < f, 0.0, close)
    swapped = f != lower
    stays[...] = jnp.where(swapped, distant[1], distant[0])
    leaves[...] = jnp.where(swapped, distant[0], distant[1])


def output_kernel(attended, weight, keep, send):
    head = lax.axis_index("head")
    width = weight.shape[0]
    for m in range(4):
        start = pl.multiple_of((head ^ m) * width, 128)
        part = dot(attended[...], weight[:, pl.ds(start, width)], ((1,), (0,)))
        if m % 2:
            send[m // 2] = part.astype(BF16)
        else:
            keep[m // 2] = part


def assemble_kernel(*refs):
    *parts, out = refs
    head = lax.axis_index("head")
    tm = lax.axis_index("tm")
    sel = (tm % 2) * 2 + (tm // 2) % 2
    row = 0
    for group, (second, others) in enumerate(((1, (2, 3)), (2, (1, 3)))):
        first_ref, second_ref, last_ref = parts[3 * group : 3 * group + 3]
        height, width = first_ref.shape
        values = {0: first_ref[...], second: second_ref[...], others[0]: last_ref[0], others[1]: last_ref[1]}
        for slot, value in values.items():
            start = pl.multiple_of((head ^ sel ^ slot) * width, 128)
            out[row : row + height, pl.ds(start, width)] = value.astype(out.dtype)
        row += height


def swap(array, axis, bit):
    return lax.ppermute(array, axis, [(i, i ^ bit) for i in range(lax.axis_size(axis))])


def local(query_rows, key_rows, value_rows, output_weight, output_grad, anchor):
    rows, cols = query_rows.shape
    heads = cols // HEAD_DIM
    frames = lax.axis_size("tm")
    seg = min(8, frames // 2)
    bounds = anchor_bounds(frames, seg)
    near_pairs = [(f - 1, f) for f in range(1, frames) if bounds[f][0] < f]
    far_frames = [f for f in range(frames) if f - bounds[f][0] >= 2]
    pair_plan = len(far_frames) == 2 and all(bounds[f][0] == bounds[f][1] for f in far_frames)

    def send(array, pairs):
        return lax.ppermute(array, "tm", pairs)

    def back(pairs):
        return [(b, a) for a, b in pairs]

    own_pair = jnp.stack([key_rows, value_rows])
    prev = send(own_pair, near_pairs)
    if pair_plan:
        lower, upper = far_frames
        source = bounds[lower][0]
        far = (
            send(own_pair, [(source, lower)]),
            send(key_rows, [(source, upper)]),
            send(prev[1], [(source + 1, upper)]),
        )
    else:
        position = lax.axis_index("tm")
        own_anchor = jnp.sum(jnp.where(jnp.arange(frames) == position, anchor, 0))
        distance = position - own_anchor
        fetched = jnp.where(distance == 0, own_pair, prev)
        step = 2
        while step < seg:
            pairs = [(f - step, f) for f in range(step, frames) if f - bounds[f][0] >= step]
            fetched = jnp.where(distance >= step, send(fetched, pairs), fetched)
            step *= 2
        far = (fetched,)

    across = swap(output_grad, "head", 2)
    columns = (output_grad, swap(output_grad, "head", 1), across, swap(across, "head", 1))
    attended_grad = pl.pallas_call(
        cotangent_kernel,
        out_shape=jax.ShapeDtypeStruct((rows, cols), BF16),
        in_specs=[vmem()] * 5,
        out_specs=vmem(),
        compiler_params=params(8),
        name="cotangent",
    )(*columns, output_weight)

    by_head = pl.BlockSpec((rows, HEAD_DIM), lambda h: (0, h))
    pair_by_head = pl.BlockSpec((2, rows, HEAD_DIM), lambda h: (0, 0, h))
    stat_spec = pl.BlockSpec((1, 8, rows), lambda h: (h, 0, 0))
    part_spec = pl.BlockSpec((1, HEAD_DIM, rows), lambda h: (h, 0, 0))
    narrow = jax.ShapeDtypeStruct((rows, cols), BF16)
    part_shape = jax.ShapeDtypeStruct((heads, HEAD_DIM, rows), F32)
    stat_shape = jax.ShapeDtypeStruct((heads, 8, rows), F32)

    count = len(far)
    near_args = (anchor, query_rows, key_rows, value_rows, prev)
    near_specs = [smem(), by_head, by_head, by_head, pair_by_head]
    far_specs = [*near_specs, pair_by_head, *[by_head] * (count - 1)]
    part, near = pl.pallas_call(
        near_kernel,
        grid=(heads,),
        out_shape=(part_shape, stat_shape),
        in_specs=near_specs,
        out_specs=(part_spec, stat_spec),
        scratch_shapes=[pltpu.VMEM((2 * rows, HEAD_DIM), BF16)] * 2,
        compiler_params=params(12),
        name="near",
    )(*near_args)

    half_spec = pl.BlockSpec((2, HEAD_DIM, cols), lambda h: (0, h, 0))
    attended, stats, keep, away = pl.pallas_call(
        functools.partial(far_kernel, count),
        grid=(heads,),
        out_shape=(
            narrow,
            stat_shape,
            jax.ShapeDtypeStruct((2, cols, cols), F32),
            jax.ShapeDtypeStruct((2, cols, cols), BF16),
        ),
        in_specs=[*far_specs, part_spec, stat_spec, by_head, *[vmem()] * 4],
        out_specs=(by_head, stat_spec, half_spec, half_spec),
        scratch_shapes=[pltpu.VMEM((4, rows, cols), BF16), pltpu.VMEM((HEAD_DIM, rows), BF16)],
        compiler_params=params(14),
        name="far",
    )(*near_args, *far, part, near, attended_grad, *columns)

    query_grad, own_grad, near_dk, near_dv, far_dv, far_dk = pl.pallas_call(
        functools.partial(backward_kernel, count, far_frames[0] if pair_plan else -1),
        grid=(heads,),
        out_shape=(narrow, jax.ShapeDtypeStruct((2, rows, cols), F32), narrow, narrow, narrow, narrow),
        in_specs=[*far_specs, by_head, stat_spec],
        out_specs=(by_head, pair_by_head, *[by_head] * 4),
        scratch_shapes=[pltpu.VMEM((3 * rows, HEAD_DIM), BF16)] * 2
        + [pltpu.VMEM((3 * rows, HEAD_DIM), F32)] * 2,
        compiler_params=params(16),
        name="backward",
    )(*near_args, *far, attended_grad, stats)

    if pair_plan:
        stays, leaves = far_dv, far_dk
        from_k = send(near_dk, back(near_pairs))
    keep_a, keep_b = keep[:, : cols // 2], keep[:, cols // 2 :]
    away_a, away_b = away[:, : cols // 2], away[:, cols // 2 :]
    if frames == 8:
        arrived_a, arrived_b = swap(away_a, "tm", 1), swap(away_b, "tm", 2)
        arrived_a, arrived_b, query_grad = lax.optimization_barrier((arrived_a, arrived_b, query_grad))
        half_a, half_b = keep_a + arrived_a.astype(F32), keep_b + arrived_b.astype(F32)
        quarter_a = half_a[0] + swap(half_a[1].astype(BF16), "tm", 2).astype(F32)
        quarter_b = half_b[0] + swap(half_b[1].astype(BF16), "tm", 1).astype(F32)
        quarter = jnp.concatenate([quarter_a, quarter_b], 0).astype(BF16)
        quarter, leaves = lax.optimization_barrier((quarter, leaves))
        crossing = send(leaves, [(lower, upper), (upper, lower)])
        merged = (stays.astype(F32) + crossing.astype(F32)).astype(BF16)
        own = (quarter.astype(F32) + swap(quarter, "tm", 4).astype(F32)).astype(BF16)
        own, merged = lax.optimization_barrier((own, merged))
        own_a, own_b = own[: cols // 2], own[cols // 2 :]
        other_a, other_b = swap(own_a, "tm", 2), swap(own_b, "tm", 1)
        sums = (
            *(own_a, other_a, swap(jnp.stack([own_a, other_a]), "tm", 1)),
            *(own_b, other_b, swap(jnp.stack([own_b, other_b]), "tm", 2)),
        )
    else:
        sums = (keep_a[0], keep_a[1], away_a.astype(F32), keep_b[0], keep_b[1], away_b.astype(F32))
    weight_grad = pl.pallas_call(
        assemble_kernel,
        out_shape=jax.ShapeDtypeStruct((cols, 4 * cols), F32),
        in_specs=[vmem()] * 6,
        out_specs=vmem(),
        compiler_params=params(8),
        name="assemble",
    )(*sums)
    if frames != 8:
        weight_grad = lax.psum(weight_grad, "tm")

    if pair_plan:
        home_k = send(merged, [(lower, source)]).astype(F32)
        home_v = send(merged, [(upper, source + 1)])
        if frames == 8:
            home_v = lax.optimization_barrier((home_v, other_a, other_b))[0]
        from_v = send((near_dv.astype(F32) + home_v.astype(F32)).astype(BF16), back(near_pairs))
        key_total = own_grad[0] + from_k.astype(F32) + home_k
        key_total, from_v = lax.optimization_barrier((key_total.astype(BF16), from_v))
        value_total = own_grad[1] + from_v.astype(F32)
    else:
        both = []
        for own, near, far in ((own_grad[0], near_dk, far_dk), (own_grad[1], near_dv, far_dv)):
            held = far.astype(F32)
            step = 2
            while 2 * step < seg:
                step *= 2
            while step >= 2:
                pairs = [(f, f - step) for f in range(step, frames) if f - bounds[f][0] >= step]
                leaving = jnp.where(distance >= step, held, 0.0)
                held = (held - leaving) + send(leaving.astype(BF16), pairs).astype(F32)
                step //= 2
            to_prev = near.astype(F32) + jnp.where(distance == 1, held, 0.0)
            from_near = send(to_prev.astype(BF16), back(near_pairs)).astype(F32)
            both.append(own + from_near + jnp.where(distance == 0, held, 0.0))
        key_total, value_total = both
    key_grad, value_grad = key_total.astype(BF16), value_total.astype(BF16)

    out_keep, out_send = pl.pallas_call(
        output_kernel,
        out_shape=(
            jax.ShapeDtypeStruct((2, rows, cols), F32),
            jax.ShapeDtypeStruct((2, rows, cols), BF16),
        ),
        in_specs=[vmem()] * 2,
        out_specs=(vmem(), vmem()),
        compiler_params=params(8),
        name="output",
    )(attended, output_weight)
    pair_sum = out_keep + swap(out_send, "head", 1).astype(F32)
    layer_output = (pair_sum[0] + swap(pair_sum[1].astype(BF16), "head", 2).astype(F32)).astype(BF16)
    return layer_output, query_grad, key_grad, value_grad, weight_grad


def solution(mesh):
    in_specs = (
        P("tm", "head"),
        P("tm", "head"),
        P("tm", "head"),
        P("head", None),
        P("tm", "head"),
        P(),
    )
    out_specs = (
        P("tm", "head"),
        P("tm", "head"),
        P("tm", "head"),
        P("tm", "head"),
        P("head", None),
    )
    return jax.shard_map(local, mesh=mesh, in_specs=in_specs, out_specs=out_specs, check_vma=False)
```

```python
import functools
import math

import jax
import jax.numpy as jnp
from jax import lax
from jax.experimental import pallas as pl
from jax.experimental.pallas import tpu as pltpu
from jax.sharding import PartitionSpec as P

HEAD_DIM = 128
BF16 = jnp.bfloat16
F32 = jnp.float32
SCALE = HEAD_DIM ** -0.5
SCALE_LOG2 = SCALE * math.log2(math.e)
Q_CHUNK = 512


def dot(a, b, dims):
    return lax.dot_general(a, b, (dims, ((), ())), preferred_element_type=F32)


def anchor_bounds(frames, seg):
    forced = frames // 2 - 2
    bounds = []
    for f in range(frames):
        if f < forced:
            bounds.append((max(0, f - seg + 1), f))
        elif f < forced + seg:
            bounds.append((forced, forced))
        else:
            bounds.append((max(forced + seg, f - seg + 1), f))
    return bounds


def vmem():
    return pl.BlockSpec(memory_space=pltpu.VMEM)


def smem():
    return pl.BlockSpec(memory_space=pltpu.SMEM)


def params(mebibytes):
    return pltpu.CompilerParams(vmem_limit_bytes=mebibytes * 1024 * 1024)


def cotangent_kernel(own, second, third, fourth, weight, out):
    head = lax.axis_index("head")
    width = own.shape[1]
    total = None
    for m, piece in enumerate((own, second, third, fourth)):
        start = pl.multiple_of((head ^ m) * width, 128)
        term = dot(piece[...], weight[:, pl.ds(start, width)], ((1,), (1,)))
        total = term if total is None else total + term
    out[...] = total.astype(BF16)


def earlier(anchor, own, prev):
    f = lax.axis_index("tm")
    return jnp.where(anchor[f] < f, prev, own[...])


def furthest(anchor, own, prev, far):
    f = lax.axis_index("tm")
    distant = far[0]
    for more in far[1:]:
        distant = distant + more
    return jnp.where(f - anchor[f] >= 2, distant, earlier(anchor, own, prev))


def distant_pair(far):
    return [far[0][0], *[x[...] for x in far[1:2]]], [far[0][1], *[x[...] for x in far[2:3]]]


def near_kernel(anchor, q, k, v, prev, part, stats, keys, values):
    rows = q.shape[0]
    keys[:rows, :] = earlier(anchor, k, prev[0])
    keys[rows:, :] = k[...]
    values[:rows, :] = earlier(anchor, v, prev[1])
    values[rows:, :] = v[...]
    for c in range(rows // Q_CHUNK):
        at = pl.ds(c * Q_CHUNK, Q_CHUNK)
        scores = dot(keys[...], q[at, :], ((1,), (1,)))
        highest = jnp.max(scores, axis=0, keepdims=True)
        raw = jnp.exp2((scores - highest) * SCALE_LOG2)
        part[0, :, at] = dot(values[...], raw.astype(BF16), ((0,), (0,)))
        stats[0, 0:1, at] = highest
        stats[0, 1:2, at] = jnp.sum(raw, axis=0, keepdims=True)


def far_kernel(count, anchor, q, k, v, prev, *rest):
    far_k, far_v = distant_pair(rest[:count])
    part, near, grad, *columns = rest[count : count + 7]
    out, stats, keep, send, pieces, turned = rest[count + 7 :]
    rows = q.shape[0]
    tm = lax.axis_index("tm")
    sel = (tm % 2) * 2 + (tm // 2) % 2

    @pl.when(pl.program_id(0) == 0)
    def _():
        for m, piece in enumerate(columns):
            pieces[m] = piece[...]

    keys = furthest(anchor, k, prev[0], far_k)
    values = furthest(anchor, v, prev[1], far_v)
    for c in range(rows // Q_CHUNK):
        at = pl.ds(c * Q_CHUNK, Q_CHUNK)
        scores = dot(keys, q[at, :], ((1,), (1,)))
        before = near[0, 0:1, at]
        highest = jnp.maximum(jnp.max(scores, axis=0, keepdims=True), before)
        raw = jnp.exp2((scores - highest) * SCALE_LOG2)
        fade = jnp.exp2((before - highest) * SCALE_LOG2)
        total = jnp.sum(raw, axis=0, keepdims=True) + near[0, 1:2, at] * fade
        attended = dot(values, raw.astype(BF16), ((0,), (0,))) + part[0, :, at] * fade
        attended = attended / total
        turned[:, at] = attended.astype(BF16)
        out[at, :] = attended.T.astype(BF16)
        delta = jnp.sum(attended * grad[at, :].astype(F32).T, axis=0, keepdims=True)
        stats[0, 0:1, at] = highest * SCALE_LOG2 + jnp.log2(total)
        stats[0, 1:2, at] = delta
    def term(slot):
        return dot(turned[...], pieces[slot ^ sel], ((1,), (0,)))

    row = pl.program_id(0) * HEAD_DIM + lax.broadcasted_iota(jnp.int32, keep.shape[1:], 0)
    upper = row < keep.shape[2] // 2
    second, third = term(1), term(2)
    send[0] = jnp.where(upper, third, second).astype(BF16)
    send[1] = term(3).astype(BF16)
    keep[0] = term(0)
    keep[1] = jnp.where(upper, second, third)


def backward_kernel(count, lower, anchor, q, k, v, prev, *rest):
    far_k, far_v = distant_pair(rest[:count])
    grad, stats, dq, own_grad, near_dk, near_dv, stays, leaves = rest[count : count + 8]
    keys, values, dk, dv = rest[count + 8 :]
    rows = q.shape[0]
    keys[:rows, :] = furthest(anchor, k, prev[0], far_k)
    keys[rows : 2 * rows, :] = earlier(anchor, k, prev[0])
    keys[2 * rows :, :] = k[...]
    values[:rows, :] = furthest(anchor, v, prev[1], far_v)
    values[rows : 2 * rows, :] = earlier(anchor, v, prev[1])
    values[2 * rows :, :] = v[...]
    for c in range(rows // Q_CHUNK):
        at = pl.ds(c * Q_CHUNK, Q_CHUNK)
        queries, cot = q[at, :], grad[at, :]
        scores = dot(keys[...], queries, ((1,), (1,)))
        prob = jnp.exp2(scores * SCALE_LOG2 - stats[0, 0:1, at])
        prob_grad = dot(values[...], cot, ((1,), (1,)))
        score_grad = (prob * (prob_grad - stats[0, 1:2, at])).astype(BF16)
        dv_term = dot(prob.astype(BF16), cot, ((1,), (0,)))
        dk_term = dot(score_grad, queries, ((1,), (0,)))
        if c == 0:
            dv[...] = dv_term
            dk[...] = dk_term
        else:
            dv[...] += dv_term
            dk[...] += dk_term
        dq_t = dot(keys[...], score_grad, ((0,), (0,))) * SCALE
        dq[at, :] = dq_t.T.astype(BF16)
    f = lax.axis_index("tm")
    a = anchor[f]
    distant = []
    for kind, (ref, near, factor) in enumerate(((dk, near_dk, SCALE), (dv, near_dv, None))):
        parts = [ref[pl.ds(block * rows, rows), :] for block in range(3)]
        if factor is not None:
            parts = [part * factor for part in parts]
        close = parts[1] + jnp.where(f - a >= 2, 0.0, parts[0])
        distant.append(jnp.where(f - a >= 2, parts[0], 0.0).astype(BF16))
        near[...] = jnp.where(a < f, close, 0.0).astype(BF16)
        own_grad[kind] = parts[2] + jnp.where(a < f, 0.0, close)
    swapped = f != lower
    stays[...] = jnp.where(swapped, distant[1], distant[0])
    leaves[...] = jnp.where(swapped, distant[0], distant[1])


def output_kernel(attended, weight, keep, send):
    head = lax.axis_index("head")
    width = weight.shape[0]
    for m in range(4):
        start = pl.multiple_of((head ^ m) * width, 128)
        part = dot(attended[...], weight[:, pl.ds(start, width)], ((1,), (0,)))
        if m % 2:
            send[m // 2] = part.astype(BF16)
        else:
            keep[m // 2] = part


def assemble_kernel(*refs):
    *parts, out = refs
    head = lax.axis_index("head")
    tm = lax.axis_index("tm")
    sel = (tm % 2) * 2 + (tm // 2) % 2
    row = 0
    for group, (second, others) in enumerate(((1, (2, 3)), (2, (1, 3)))):
        first_ref, second_ref, last_ref = parts[3 * group : 3 * group + 3]
        height, width = first_ref.shape
        values = {0: first_ref[...], second: second_ref[...], others[0]: last_ref[0], others[1]: last_ref[1]}
        for slot, value in values.items():
            start = pl.multiple_of((head ^ sel ^ slot) * width, 128)
            out[row : row + height, pl.ds(start, width)] = value.astype(out.dtype)
        row += height


def swap(array, axis, bit):
    return lax.ppermute(array, axis, [(i, i ^ bit) for i in range(lax.axis_size(axis))])


def local(query_rows, key_rows, value_rows, output_weight, output_grad, anchor):
    rows, cols = query_rows.shape
    heads = cols // HEAD_DIM
    frames = lax.axis_size("tm")
    seg = min(8, frames // 2)
    bounds = anchor_bounds(frames, seg)
    near_pairs = [(f - 1, f) for f in range(1, frames) if bounds[f][0] < f]
    far_frames = [f for f in range(frames) if f - bounds[f][0] >= 2]
    pair_plan = len(far_frames) == 2 and all(bounds[f][0] == bounds[f][1] for f in far_frames)

    def send(array, pairs):
        return lax.ppermute(array, "tm", pairs)

    def back(pairs):
        return [(b, a) for a, b in pairs]

    own_pair = jnp.stack([key_rows, value_rows])
    prev = send(own_pair, near_pairs)
    if pair_plan:
        lower, upper = far_frames
        source = bounds[lower][0]
        far = (
            send(own_pair, [(source, lower)]),
            send(key_rows, [(source, upper)]),
            send(prev[1], [(source + 1, upper)]),
        )
    else:
        position = lax.axis_index("tm")
        own_anchor = jnp.sum(jnp.where(jnp.arange(frames) == position, anchor, 0))
        distance = position - own_anchor
        fetched = jnp.where(distance == 0, own_pair, prev)
        step = 2
        while step < seg:
            pairs = [(f - step, f) for f in range(step, frames) if f - bounds[f][0] >= step]
            fetched = jnp.where(distance >= step, send(fetched, pairs), fetched)
            step *= 2
        far = (fetched,)

    across = swap(output_grad, "head", 2)
    columns = (output_grad, swap(output_grad, "head", 1), across, swap(across, "head", 1))
    attended_grad = pl.pallas_call(
        cotangent_kernel,
        out_shape=jax.ShapeDtypeStruct((rows, cols), BF16),
        in_specs=[vmem()] * 5,
        out_specs=vmem(),
        compiler_params=params(8),
        name="cotangent",
    )(*columns, output_weight)

    by_head = pl.BlockSpec((rows, HEAD_DIM), lambda h: (0, h))
    pair_by_head = pl.BlockSpec((2, rows, HEAD_DIM), lambda h: (0, 0, h))
    stat_spec = pl.BlockSpec((1, 8, rows), lambda h: (h, 0, 0))
    part_spec = pl.BlockSpec((1, HEAD_DIM, rows), lambda h: (h, 0, 0))
    narrow = jax.ShapeDtypeStruct((rows, cols), BF16)
    part_shape = jax.ShapeDtypeStruct((heads, HEAD_DIM, rows), F32)
    stat_shape = jax.ShapeDtypeStruct((heads, 8, rows), F32)

    count = len(far)
    near_args = (anchor, query_rows, key_rows, value_rows, prev)
    near_specs = [smem(), by_head, by_head, by_head, pair_by_head]
    far_specs = [*near_specs, pair_by_head, *[by_head] * (count - 1)]
    part, near = pl.pallas_call(
        near_kernel,
        grid=(heads,),
        out_shape=(part_shape, stat_shape),
        in_specs=near_specs,
        out_specs=(part_spec, stat_spec),
        scratch_shapes=[pltpu.VMEM((2 * rows, HEAD_DIM), BF16)] * 2,
        compiler_params=params(12),
        name="near",
    )(*near_args)

    half_spec = pl.BlockSpec((2, HEAD_DIM, cols), lambda h: (0, h, 0))
    attended, stats, keep, away = pl.pallas_call(
        functools.partial(far_kernel, count),
        grid=(heads,),
        out_shape=(
            narrow,
            stat_shape,
            jax.ShapeDtypeStruct((2, cols, cols), F32),
            jax.ShapeDtypeStruct((2, cols, cols), BF16),
        ),
        in_specs=[*far_specs, part_spec, stat_spec, by_head, *[vmem()] * 4],
        out_specs=(by_head, stat_spec, half_spec, half_spec),
        scratch_shapes=[pltpu.VMEM((4, rows, cols), BF16), pltpu.VMEM((HEAD_DIM, rows), BF16)],
        compiler_params=params(14),
        name="far",
    )(*near_args, *far, part, near, attended_grad, *columns)

    query_grad, own_grad, near_dk, near_dv, far_dv, far_dk = pl.pallas_call(
        functools.partial(backward_kernel, count, far_frames[0] if pair_plan else -1),
        grid=(heads,),
        out_shape=(narrow, jax.ShapeDtypeStruct((2, rows, cols), F32), narrow, narrow, narrow, narrow),
        in_specs=[*far_specs, by_head, stat_spec],
        out_specs=(by_head, pair_by_head, *[by_head] * 4),
        scratch_shapes=[pltpu.VMEM((3 * rows, HEAD_DIM), BF16)] * 2
        + [pltpu.VMEM((3 * rows, HEAD_DIM), F32)] * 2,
        compiler_params=params(16),
        name="backward",
    )(*near_args, *far, attended_grad, stats)

    if pair_plan:
        stays, leaves = far_dv, far_dk
        from_k = send(near_dk, back(near_pairs))
    keep_a, keep_b = keep[:, : cols // 2], keep[:, cols // 2 :]
    away_a, away_b = away[:, : cols // 2], away[:, cols // 2 :]
    if frames == 8:
        arrived_a, arrived_b = swap(away_a, "tm", 1), swap(away_b, "tm", 2)
        arrived_a, arrived_b, query_grad = lax.optimization_barrier((arrived_a, arrived_b, query_grad))
        half_a, half_b = keep_a + arrived_a.astype(F32), keep_b + arrived_b.astype(F32)
        quarter_a = half_a[0] + swap(half_a[1].astype(BF16), "tm", 2).astype(F32)
        quarter_b = half_b[0] + swap(half_b[1].astype(BF16), "tm", 1).astype(F32)
        quarter = jnp.concatenate([quarter_a, quarter_b], 0).astype(BF16)
        quarter, leaves = lax.optimization_barrier((quarter, leaves))
        crossing = send(leaves, [(lower, upper), (upper, lower)])
        merged = (stays.astype(F32) + crossing.astype(F32)).astype(BF16)
        own = (quarter.astype(F32) + swap(quarter, "tm", 4).astype(F32)).astype(BF16)
        own, merged = lax.optimization_barrier((own, merged))
        own_a, own_b = own[: cols // 2], own[cols // 2 :]
        other_a, other_b = swap(own_a, "tm", 2), swap(own_b, "tm", 1)
        sums = (
            *(own_a, other_a, swap(jnp.stack([own_a, other_a]), "tm", 1)),
            *(own_b, other_b, swap(jnp.stack([own_b, other_b]), "tm", 2)),
        )
    else:
        sums = (keep_a[0], keep_a[1], away_a.astype(F32), keep_b[0], keep_b[1], away_b.astype(F32))
    weight_grad = pl.pallas_call(
        assemble_kernel,
        out_shape=jax.ShapeDtypeStruct((cols, 4 * cols), F32),
        in_specs=[vmem()] * 6,
        out_specs=vmem(),
        compiler_params=params(8),
        name="assemble",
    )(*sums)
    if frames != 8:
        weight_grad = lax.psum(weight_grad, "tm")

    if pair_plan:
        home_k = send(merged, [(lower, source)]).astype(F32)
        home_v = send(merged, [(upper, source + 1)])
        if frames == 8:
            home_v = lax.optimization_barrier((home_v, other_a, other_b))[0]
        from_v = send((near_dv.astype(F32) + home_v.astype(F32)).astype(BF16), back(near_pairs))
        key_total = own_grad[0] + from_k.astype(F32) + home_k
        key_total, from_v = lax.optimization_barrier((key_total.astype(BF16), from_v))
        value_total = own_grad[1] + from_v.astype(F32)
    else:
        both = []
        for own, near, far in ((own_grad[0], near_dk, far_dk), (own_grad[1], near_dv, far_dv)):
            held = far.astype(F32)
            step = 2
            while 2 * step < seg:
                step *= 2
            while step >= 2:
                pairs = [(f, f - step) for f in range(step, frames) if f - bounds[f][0] >= step]
                leaving = jnp.where(distance >= step, held, 0.0)
                held = (held - leaving) + send(leaving.astype(BF16), pairs).astype(F32)
                step //= 2
            to_prev = near.astype(F32) + jnp.where(distance == 1, held, 0.0)
            from_near = send(to_prev.astype(BF16), back(near_pairs)).astype(F32)
            both.append(own + from_near + jnp.where(distance == 0, held, 0.0))
        key_total, value_total = both
    key_grad, value_grad = key_total.astype(BF16), value_total.astype(BF16)

    if pair_plan and frames == 8:
        attended = lax.optimization_barrier((attended, leaves))[0]
    out_keep, out_send = pl.pallas_call(
        output_kernel,
        out_shape=(
            jax.ShapeDtypeStruct((2, rows, cols), F32),
            jax.ShapeDtypeStruct((2, rows, cols), BF16),
        ),
        in_specs=[vmem()] * 2,
        out_specs=(vmem(), vmem()),
        compiler_params=params(8),
        name="output",
    )(attended, output_weight)
    pair_sum = out_keep + swap(out_send, "head", 1).astype(F32)
    layer_output = (pair_sum[0] + swap(pair_sum[1].astype(BF16), "head", 2).astype(F32)).astype(BF16)
    return layer_output, query_grad, key_grad, value_grad, weight_grad


def solution(mesh):
    in_specs = (
        P("tm", "head"),
        P("tm", "head"),
        P("tm", "head"),
        P("head", None),
        P("tm", "head"),
        P(),
    )
    out_specs = (
        P("tm", "head"),
        P("tm", "head"),
        P("tm", "head"),
        P("tm", "head"),
        P("head", None),
    )
    return jax.shard_map(local, mesh=mesh, in_specs=in_specs, out_specs=out_specs, check_vma=False)
```

```python
import functools
import math

import jax
import jax.numpy as jnp
from jax import lax
from jax.experimental import pallas as pl
from jax.experimental.pallas import tpu as pltpu
from jax.sharding import PartitionSpec as P

HEAD_DIM = 128
BF16 = jnp.bfloat16
F32 = jnp.float32
SCALE = HEAD_DIM ** -0.5
SCALE_LOG2 = SCALE * math.log2(math.e)
Q_CHUNK = 512


def dot(a, b, dims):
    return lax.dot_general(a, b, (dims, ((), ())), preferred_element_type=F32)


def anchor_bounds(frames, seg):
    forced = frames // 2 - 2
    bounds = []
    for f in range(frames):
        if f < forced:
            bounds.append((max(0, f - seg + 1), f))
        elif f < forced + seg:
            bounds.append((forced, forced))
        else:
            bounds.append((max(forced + seg, f - seg + 1), f))
    return bounds


def vmem():
    return pl.BlockSpec(memory_space=pltpu.VMEM)


def smem():
    return pl.BlockSpec(memory_space=pltpu.SMEM)


def params(mebibytes):
    return pltpu.CompilerParams(vmem_limit_bytes=mebibytes * 1024 * 1024)


def cotangent_kernel(own, second, third, fourth, weight, out):
    head = lax.axis_index("head")
    width = own.shape[1]
    total = None
    for m, piece in enumerate((own, second, third, fourth)):
        start = pl.multiple_of((head ^ m) * width, 128)
        term = dot(piece[...], weight[:, pl.ds(start, width)], ((1,), (1,)))
        total = term if total is None else total + term
    out[...] = total.astype(BF16)


def earlier(anchor, own, prev):
    f = lax.axis_index("tm")
    return jnp.where(anchor[f] < f, prev, own[...])


def furthest(anchor, own, prev, far):
    f = lax.axis_index("tm")
    distant = far[0]
    for more in far[1:]:
        distant = distant + more
    return jnp.where(f - anchor[f] >= 2, distant, earlier(anchor, own, prev))


def distant_pair(far):
    return [far[0][0], *[x[...] for x in far[1:2]]], [far[0][1], *[x[...] for x in far[2:3]]]


def near_kernel(anchor, q, k, v, prev, part, stats, keys, values):
    rows = q.shape[0]
    keys[:rows, :] = earlier(anchor, k, prev[0])
    keys[rows:, :] = k[...]
    values[:rows, :] = earlier(anchor, v, prev[1])
    values[rows:, :] = v[...]
    for c in range(rows // Q_CHUNK):
        at = pl.ds(c * Q_CHUNK, Q_CHUNK)
        scores = dot(keys[...], q[at, :], ((1,), (1,)))
        highest = jnp.max(scores, axis=0, keepdims=True)
        raw = jnp.exp2((scores - highest) * SCALE_LOG2)
        part[0, :, at] = dot(values[...], raw.astype(BF16), ((0,), (0,)))
        stats[0, 0:1, at] = highest
        stats[0, 1:2, at] = jnp.sum(raw, axis=0, keepdims=True)


def far_kernel(count, anchor, q, k, v, prev, *rest):
    far_k, far_v = distant_pair(rest[:count])
    part, near, grad, *columns = rest[count : count + 7]
    out, stats, keep, send, pieces, turned = rest[count + 7 :]
    rows = q.shape[0]
    tm = lax.axis_index("tm")
    sel = (tm % 2) * 2 + (tm // 2) % 2

    @pl.when(pl.program_id(0) == 0)
    def _():
        for m, piece in enumerate(columns):
            pieces[m] = piece[...]

    keys = furthest(anchor, k, prev[0], far_k)
    values = furthest(anchor, v, prev[1], far_v)
    for c in range(rows // Q_CHUNK):
        at = pl.ds(c * Q_CHUNK, Q_CHUNK)
        scores = dot(keys, q[at, :], ((1,), (1,)))
        before = near[0, 0:1, at]
        highest = jnp.maximum(jnp.max(scores, axis=0, keepdims=True), before)
        raw = jnp.exp2((scores - highest) * SCALE_LOG2)
        fade = jnp.exp2((before - highest) * SCALE_LOG2)
        total = jnp.sum(raw, axis=0, keepdims=True) + near[0, 1:2, at] * fade
        attended = dot(values, raw.astype(BF16), ((0,), (0,))) + part[0, :, at] * fade
        attended = attended / total
        turned[:, at] = attended.astype(BF16)
        out[at, :] = attended.T.astype(BF16)
        delta = jnp.sum(attended * grad[at, :].astype(F32).T, axis=0, keepdims=True)
        stats[0, 0:1, at] = highest * SCALE_LOG2 + jnp.log2(total)
        stats[0, 1:2, at] = delta
    def term(slot):
        return dot(turned[...], pieces[slot ^ sel], ((1,), (0,)))

    row = pl.program_id(0) * HEAD_DIM + lax.broadcasted_iota(jnp.int32, keep.shape[1:], 0)
    upper = row < keep.shape[2] // 2
    second, third = term(1), term(2)
    send[0] = jnp.where(upper, third, second).astype(BF16)
    send[1] = term(3).astype(BF16)
    keep[0] = term(0)
    keep[1] = jnp.where(upper, second, third)


def backward_kernel(count, lower, anchor, q, k, v, prev, *rest):
    far_k, far_v = distant_pair(rest[:count])
    grad, stats, dq, own_grad, near_dk, near_dv, stays, leaves = rest[count : count + 8]
    keys, values, dk, dv = rest[count + 8 :]
    rows = q.shape[0]
    keys[:rows, :] = furthest(anchor, k, prev[0], far_k)
    keys[rows : 2 * rows, :] = earlier(anchor, k, prev[0])
    keys[2 * rows :, :] = k[...]
    values[:rows, :] = furthest(anchor, v, prev[1], far_v)
    values[rows : 2 * rows, :] = earlier(anchor, v, prev[1])
    values[2 * rows :, :] = v[...]
    for c in range(rows // Q_CHUNK):
        at = pl.ds(c * Q_CHUNK, Q_CHUNK)
        queries, cot = q[at, :], grad[at, :]
        scores = dot(keys[...], queries, ((1,), (1,)))
        prob = jnp.exp2(scores * SCALE_LOG2 - stats[0, 0:1, at])
        prob_grad = dot(values[...], cot, ((1,), (1,)))
        score_grad = (prob * (prob_grad - stats[0, 1:2, at])).astype(BF16)
        dv_term = dot(prob.astype(BF16), cot, ((1,), (0,)))
        dk_term = dot(score_grad, queries, ((1,), (0,)))
        if c == 0:
            dv[...] = dv_term
            dk[...] = dk_term
        else:
            dv[...] += dv_term
            dk[...] += dk_term
        dq_t = dot(keys[...], score_grad, ((0,), (0,))) * SCALE
        dq[at, :] = dq_t.T.astype(BF16)
    f = lax.axis_index("tm")
    a = anchor[f]
    distant = []
    for kind, (ref, near, factor) in enumerate(((dk, near_dk, SCALE), (dv, near_dv, None))):
        parts = [ref[pl.ds(block * rows, rows), :] for block in range(3)]
        if factor is not None:
            parts = [part * factor for part in parts]
        close = parts[1] + jnp.where(f - a >= 2, 0.0, parts[0])
        distant.append(jnp.where(f - a >= 2, parts[0], 0.0).astype(BF16))
        near[...] = jnp.where(a < f, close, 0.0).astype(BF16)
        own_grad[kind] = parts[2] + jnp.where(a < f, 0.0, close)
    swapped = f != lower
    stays[...] = jnp.where(swapped, distant[1], distant[0])
    leaves[...] = jnp.where(swapped, distant[0], distant[1])


def output_kernel(attended, weight, keep, send):
    head = lax.axis_index("head")
    width = weight.shape[0]
    for m in range(4):
        start = pl.multiple_of((head ^ m) * width, 128)
        part = dot(attended[...], weight[:, pl.ds(start, width)], ((1,), (0,)))
        if m % 2:
            send[m // 2] = part.astype(BF16)
        else:
            keep[m // 2] = part


def assemble_kernel(*refs):
    *parts, out = refs
    head = lax.axis_index("head")
    tm = lax.axis_index("tm")
    sel = (tm % 2) * 2 + (tm // 2) % 2
    row = 0
    for group, (second, others) in enumerate(((1, (2, 3)), (2, (1, 3)))):
        first_ref, second_ref, last_ref = parts[3 * group : 3 * group + 3]
        height, width = first_ref.shape
        values = {0: first_ref[...], second: second_ref[...], others[0]: last_ref[0], others[1]: last_ref[1]}
        for slot, value in values.items():
            start = pl.multiple_of((head ^ sel ^ slot) * width, 128)
            out[row : row + height, pl.ds(start, width)] = value.astype(out.dtype)
        row += height


def swap(array, axis, bit):
    return lax.ppermute(array, axis, [(i, i ^ bit) for i in range(lax.axis_size(axis))])


def local(query_rows, key_rows, value_rows, output_weight, output_grad, anchor):
    rows, cols = query_rows.shape
    heads = cols // HEAD_DIM
    frames = lax.axis_size("tm")
    seg = min(8, frames // 2)
    bounds = anchor_bounds(frames, seg)
    near_pairs = [(f - 1, f) for f in range(1, frames) if bounds[f][0] < f]
    far_frames = [f for f in range(frames) if f - bounds[f][0] >= 2]
    pair_plan = len(far_frames) == 2 and all(bounds[f][0] == bounds[f][1] for f in far_frames)

    def send(array, pairs):
        return lax.ppermute(array, "tm", pairs)

    def back(pairs):
        return [(b, a) for a, b in pairs]

    own_pair = jnp.stack([key_rows, value_rows])
    prev = send(own_pair, near_pairs)
    if pair_plan:
        lower, upper = far_frames
        source = bounds[lower][0]
        far = (
            send(own_pair, [(source, lower)]),
            send(key_rows, [(source, upper)]),
            send(prev[1], [(source + 1, upper)]),
        )
    else:
        position = lax.axis_index("tm")
        own_anchor = jnp.sum(jnp.where(jnp.arange(frames) == position, anchor, 0))
        distance = position - own_anchor
        fetched = jnp.where(distance == 0, own_pair, prev)
        step = 2
        while step < seg:
            pairs = [(f - step, f) for f in range(step, frames) if f - bounds[f][0] >= step]
            fetched = jnp.where(distance >= step, send(fetched, pairs), fetched)
            step *= 2
        far = (fetched,)

    across = swap(output_grad, "head", 2)
    columns = (output_grad, swap(output_grad, "head", 1), across, swap(across, "head", 1))
    attended_grad = pl.pallas_call(
        cotangent_kernel,
        out_shape=jax.ShapeDtypeStruct((rows, cols), BF16),
        in_specs=[vmem()] * 5,
        out_specs=vmem(),
        compiler_params=params(8),
        name="cotangent",
    )(*columns, output_weight)

    by_head = pl.BlockSpec((rows, HEAD_DIM), lambda h: (0, h))
    pair_by_head = pl.BlockSpec((2, rows, HEAD_DIM), lambda h: (0, 0, h))
    stat_spec = pl.BlockSpec((1, 8, rows), lambda h: (h, 0, 0))
    part_spec = pl.BlockSpec((1, HEAD_DIM, rows), lambda h: (h, 0, 0))
    narrow = jax.ShapeDtypeStruct((rows, cols), BF16)
    part_shape = jax.ShapeDtypeStruct((heads, HEAD_DIM, rows), F32)
    stat_shape = jax.ShapeDtypeStruct((heads, 8, rows), F32)

    count = len(far)
    near_args = (anchor, query_rows, key_rows, value_rows, prev)
    near_specs = [smem(), by_head, by_head, by_head, pair_by_head]
    far_specs = [*near_specs, pair_by_head, *[by_head] * (count - 1)]
    part, near = pl.pallas_call(
        near_kernel,
        grid=(heads,),
        out_shape=(part_shape, stat_shape),
        in_specs=near_specs,
        out_specs=(part_spec, stat_spec),
        scratch_shapes=[pltpu.VMEM((2 * rows, HEAD_DIM), BF16)] * 2,
        compiler_params=params(12),
        name="near",
    )(*near_args)

    half_spec = pl.BlockSpec((2, HEAD_DIM, cols), lambda h: (0, h, 0))
    attended, stats, keep, away = pl.pallas_call(
        functools.partial(far_kernel, count),
        grid=(heads,),
        out_shape=(
            narrow,
            stat_shape,
            jax.ShapeDtypeStruct((2, cols, cols), F32),
            jax.ShapeDtypeStruct((2, cols, cols), BF16),
        ),
        in_specs=[*far_specs, part_spec, stat_spec, by_head, *[vmem()] * 4],
        out_specs=(by_head, stat_spec, half_spec, half_spec),
        scratch_shapes=[pltpu.VMEM((4, rows, cols), BF16), pltpu.VMEM((HEAD_DIM, rows), BF16)],
        compiler_params=params(14),
        name="far",
    )(*near_args, *far, part, near, attended_grad, *columns)

    query_grad, own_grad, near_dk, near_dv, far_dv, far_dk = pl.pallas_call(
        functools.partial(backward_kernel, count, far_frames[0] if pair_plan else -1),
        grid=(heads,),
        out_shape=(narrow, jax.ShapeDtypeStruct((2, rows, cols), F32), narrow, narrow, narrow, narrow),
        in_specs=[*far_specs, by_head, stat_spec],
        out_specs=(by_head, pair_by_head, *[by_head] * 4),
        scratch_shapes=[pltpu.VMEM((3 * rows, HEAD_DIM), BF16)] * 2
        + [pltpu.VMEM((3 * rows, HEAD_DIM), F32)] * 2,
        compiler_params=params(16),
        name="backward",
    )(*near_args, *far, attended_grad, stats)

    if pair_plan:
        stays, leaves = far_dv, far_dk
        from_k = send(near_dk, back(near_pairs))
    keep_a, keep_b = keep[:, : cols // 2], keep[:, cols // 2 :]
    away_a, away_b = away[:, : cols // 2], away[:, cols // 2 :]
    if frames == 8:
        arrived_a, arrived_b = swap(away_a, "tm", 1), swap(away_b, "tm", 2)
        arrived_a, arrived_b, query_grad = lax.optimization_barrier((arrived_a, arrived_b, query_grad))
        half_a, half_b = keep_a + arrived_a.astype(F32), keep_b + arrived_b.astype(F32)
        quarter_a = half_a[0] + swap(half_a[1].astype(BF16), "tm", 2).astype(F32)
        quarter_b = half_b[0] + swap(half_b[1].astype(BF16), "tm", 1).astype(F32)
        quarter = jnp.concatenate([quarter_a, quarter_b], 0).astype(BF16)
        quarter, leaves = lax.optimization_barrier((quarter, leaves))
        crossing = send(leaves, [(lower, upper), (upper, lower)])
        merged = (stays.astype(F32) + crossing.astype(F32)).astype(BF16)
        own = (quarter.astype(F32) + swap(quarter, "tm", 4).astype(F32)).astype(BF16)
        own, merged = lax.optimization_barrier((own, merged))
        own_a, own_b = own[: cols // 2], own[cols // 2 :]
        other_a, other_b = swap(own_a, "tm", 2), swap(own_b, "tm", 1)
        sums = (
            *(own_a, other_a, swap(jnp.stack([own_a, other_a]), "tm", 1)),
            *(own_b, other_b, swap(jnp.stack([own_b, other_b]), "tm", 2)),
        )
    else:
        sums = (keep_a[0], keep_a[1], away_a.astype(F32), keep_b[0], keep_b[1], away_b.astype(F32))
    weight_grad = pl.pallas_call(
        assemble_kernel,
        out_shape=jax.ShapeDtypeStruct((cols, 4 * cols), F32),
        in_specs=[vmem()] * 6,
        out_specs=vmem(),
        compiler_params=params(8),
        name="assemble",
    )(*sums)
    if frames != 8:
        weight_grad = lax.psum(weight_grad, "tm")

    if pair_plan:
        home_k = send(merged, [(lower, source)]).astype(F32)
        home_v = send(merged, [(upper, source + 1)])
        if frames == 8:
            home_v = lax.optimization_barrier((home_v, other_a))[0]
        from_v = send((near_dv.astype(F32) + home_v.astype(F32)).astype(BF16), back(near_pairs))
        key_total = own_grad[0] + from_k.astype(F32) + home_k
        key_total, from_v = lax.optimization_barrier((key_total.astype(BF16), from_v))
        value_total = own_grad[1] + from_v.astype(F32)
    else:
        both = []
        for own, near, far in ((own_grad[0], near_dk, far_dk), (own_grad[1], near_dv, far_dv)):
            held = far.astype(F32)
            step = 2
            while 2 * step < seg:
                step *= 2
            while step >= 2:
                pairs = [(f, f - step) for f in range(step, frames) if f - bounds[f][0] >= step]
                leaving = jnp.where(distance >= step, held, 0.0)
                held = (held - leaving) + send(leaving.astype(BF16), pairs).astype(F32)
                step //= 2
            to_prev = near.astype(F32) + jnp.where(distance == 1, held, 0.0)
            from_near = send(to_prev.astype(BF16), back(near_pairs)).astype(F32)
            both.append(own + from_near + jnp.where(distance == 0, held, 0.0))
        key_total, value_total = both
    key_grad, value_grad = key_total.astype(BF16), value_total.astype(BF16)

    if pair_plan and frames == 8:
        attended = lax.optimization_barrier((attended, leaves))[0]
    out_keep, out_send = pl.pallas_call(
        output_kernel,
        out_shape=(
            jax.ShapeDtypeStruct((2, rows, cols), F32),
            jax.ShapeDtypeStruct((2, rows, cols), BF16),
        ),
        in_specs=[vmem()] * 2,
        out_specs=(vmem(), vmem()),
        compiler_params=params(8),
        name="output",
    )(attended, output_weight)
    pair_sum = out_keep + swap(out_send, "head", 1).astype(F32)
    layer_output = (pair_sum[0] + swap(pair_sum[1].astype(BF16), "head", 2).astype(F32)).astype(BF16)
    return layer_output, query_grad, key_grad, value_grad, weight_grad


def solution(mesh):
    in_specs = (
        P("tm", "head"),
        P("tm", "head"),
        P("tm", "head"),
        P("head", None),
        P("tm", "head"),
        P(),
    )
    out_specs = (
        P("tm", "head"),
        P("tm", "head"),
        P("tm", "head"),
        P("tm", "head"),
        P("head", None),
    )
    return jax.shard_map(local, mesh=mesh, in_specs=in_specs, out_specs=out_specs, check_vma=False)
```
